32 devices in a mesh: groups: 2 (over x), seg: 16 (over z, y, core).
Axes of the slice: x: 2, y: 2, z: 4, core: 2. Of those that a mesh axis runs over, the one named last changes fastest.
Arguments:
- bins: bfloat16 [1024, 128], P(('groups', 'seg')), parts along dimension 0, may hold values from -6 to 6
- conv_weight: bfloat16 [3, 128, 128], replicated, may hold values from -0.3125 to 0.3125
- conv_bias: float32 [128], replicated, may hold values from -3 to 3
- pair_left: bfloat16 [128, 48], replicated, may hold values from -0.5 to 0.5
- pair_right: bfloat16 [128, 48], replicated, may hold values from -0.5 to 0.5
- pair_weight: bfloat16 [3, 3, 48, 48], replicated, may hold values from -0.3125 to 0.3125
- pair_bias: float32 [48], replicated, may hold values from -3 to 3
- head: bfloat16 [48], replicated, may hold values from -0.875 to 0.875
- shifts: int32 [4], replicated, may hold values from -8 to 8, as said below
- flags: int32 [4], replicated, may hold values from 0 to 1, as said below
- dilations: int32 [2], replicated, may hold values from 1 to 4, as said below
Outputs:
- contacts: float32 [1024, 512], P(('groups', 'seg')), parts along dimension 0
The draws below stay inside these ranges and needn't reach their ends.
There are 2 independent parts, one for each index of `groups`. The reference program is written for one: setup_inputs(seed, part) draws one part's arguments, and reference() takes and returns one part's arrays. A program takes and returns all parts, laid end to end along the dimension named above; an argument that names none is the same for every part. Nothing has to cross between parts.
Inputs may be any that keep to these rules, and one draw needn't show every extreme that they name: `shifts`: the largest entry is 8 and the smallest -8. `flags`: exactly half of the views are reverse-complemented. `dilations`: one of the two rates equals 4 and the other is smaller.
All inputs are finite; a program needn't handle non-finite values.
Results may differ from the reference program's by a relative error of at most 0.0055.
Values may be sent and summed in bfloat16 or wider, within the bound.
A program may use at most 128 MiB of HBM per device.

```python
import jax
import jax.numpy as jnp
from jax import lax

CHANNELS = 128
PAIR_CH = 48
BAND = 512
VIEWS = 4
SHIFT = 8
DMAX = 4
LBINS = 512
HALO = 12


def draw_shifts(key, part):
    first_key, second_key = jax.random.split(jax.random.fold_in(key, 11))
    values = jax.random.randint(first_key, (VIEWS,), -SHIFT, SHIFT + 1)
    order = jax.random.permutation(second_key, VIEWS)
    values = values.at[order[0]].set(SHIFT)
    values = values.at[order[1]].set(-SHIFT)
    return values.astype(jnp.int32)


def draw_flags(key, part):
    order = jax.random.permutation(jax.random.fold_in(key, 23), VIEWS)
    return (order % 2).astype(jnp.int32)


def draw_dilations(key, part):
    first_key, second_key = jax.random.split(jax.random.fold_in(key, 37))
    others = jax.random.randint(first_key, (2,), 1, DMAX)
    which = jax.random.randint(second_key, (), 0, 2)
    return jnp.where(jnp.arange(2) == which, DMAX, others).astype(jnp.int32)


def block_levels(key, dims, cuts, least, top_value):
    def one(dim, parts):
        draws = jax.random.uniform(jax.random.fold_in(jax.random.fold_in(key, 6), dim), (parts,), jnp.float32, least / len(cuts), top_value / len(cuts))
        return jnp.repeat(jnp.exp(draws), dims[dim] // parts).reshape((-1,) + (1,) * (len(dims) - dim - 1))

    gain = one(*cuts[0])
    for cut in cuts[1:]:
        gain = gain * one(*cut)
    return gain


def gaussian(key, extent, scale, bound, cuts=(), kind=jnp.bfloat16):
    result = scale * jax.random.normal(key, extent, jnp.float32)
    if cuts:
        result = result * block_levels(key, extent, cuts, -0.22, 0.18)
    return jnp.clip(result, -bound, bound).astype(kind)


def setup_inputs(seed: int = 0, part: int = 0) -> dict:
    streams_of = jax.random.split(jax.random.key(seed), 12)
    own_keys = jax.random.split(jax.random.fold_in(streams_of[11], part), 12)
    return {
        "bins": gaussian(own_keys[0], (LBINS, CHANNELS), 1.0, 6.0, ((0, 16),)),
        "conv_weight": gaussian(streams_of[1], (3, CHANNELS, CHANNELS), (3 * CHANNELS) ** -0.5, 0.3125),
        "conv_bias": gaussian(streams_of[2], (CHANNELS,), 0.5, 3.0, (), jnp.float32),
        "pair_left": gaussian(streams_of[3], (CHANNELS, PAIR_CH), CHANNELS ** -0.5, 0.5),
        "pair_right": gaussian(streams_of[4], (CHANNELS, PAIR_CH), CHANNELS ** -0.5, 0.5),
        "pair_weight": gaussian(streams_of[5], (3, 3, PAIR_CH, PAIR_CH), (9 * PAIR_CH) ** -0.5, 0.3125),
        "pair_bias": gaussian(streams_of[6], (PAIR_CH,), 0.5, 3.0, (), jnp.float32),
        "head": gaussian(streams_of[7], (PAIR_CH,), PAIR_CH ** -0.5, 0.875),
        "shifts": draw_shifts(jax.random.fold_in(streams_of[11], 71), part),
        "flags": draw_flags(jax.random.fold_in(streams_of[11], 71), part),
        "dilations": draw_dilations(jax.random.fold_in(streams_of[11], 71), part),
    }


block_rows = 256


def view_kernels(conv_weight, flags):
    flipped = conv_weight[::-1, ::-1, :]
    chosen = (flags == 1)[:, None, None, None]
    return jnp.where(chosen, flipped[None], conv_weight[None])


def trunk(source, base, rows, shifts, dilate_seq, kernels, conv_bias, pair_left, pair_right):
    def one_view(shift, kernel):
        start = base + shift
        taps = [lax.dynamic_slice_in_dim(source, start + (tap - 1) * dilate_seq, rows, 0) for tap in range(3)]
        mixed = jnp.zeros((rows, CHANNELS), jnp.float32)
        for tap in range(3):
            mixed = mixed + jnp.dot(taps[tap].astype(jnp.float32), kernel[tap].astype(jnp.float32))
        return taps[1], mixed

    centers, mixed = jax.vmap(one_view)(shifts, kernels)
    feature = (centers.astype(jnp.float32) + jax.nn.relu(mixed + conv_bias)).astype(jnp.bfloat16)
    left = jnp.einsum("vrc,cp->vrp", feature.astype(jnp.float32), pair_left.astype(jnp.float32)).astype(jnp.bfloat16)
    right = jnp.einsum("vrc,cp->vrp", feature.astype(jnp.float32), pair_right.astype(jnp.float32)).astype(jnp.bfloat16)
    return left, right


def pair_block(left_rows, right_rows, first_row, total, dilate_pair, pair_weight, pair_bias, head):
    span = left_rows.shape[1]
    rows_out = span - 2 * DMAX
    width = right_rows.shape[1]
    global_rows = first_row + jnp.arange(span, dtype=jnp.int32)
    offsets = jnp.arange(BAND, dtype=jnp.int32)
    inside = ((global_rows >= 0) & (global_rows < total))[:, None] & ((global_rows[:, None] + offsets[None, :]) < total)
    stacked_weight = pair_weight.reshape(9 * PAIR_CH, PAIR_CH)

    def view_step(view, running):
        left = left_rows[view]
        right_cols = right_rows[view].T
        skewed = jnp.tile(right_cols, (1, span + 1))[:, : span * (width + 1)]
        skewed = skewed.reshape(PAIR_CH, span, width + 1)[:, :, :BAND]
        pairs = jax.nn.relu(left.T.astype(jnp.float32)[:, :, None] + skewed.astype(jnp.float32))
        pairs = jnp.where(inside[None], pairs, 0.0).astype(jnp.bfloat16)
        padded = jnp.pad(pairs, ((0, 0), (0, 0), (DMAX, DMAX)))
        pieces = []
        for row_tap in range(3):
            for col_tap in range(3):
                row_start = (DMAX + (row_tap - 1) * dilate_pair).astype(jnp.int32)
                col_start = (DMAX + (col_tap - 1) * dilate_pair).astype(jnp.int32)
                pieces.append(lax.dynamic_slice(padded, (jnp.int32(0), row_start, col_start), (PAIR_CH, rows_out, BAND)))
        stacked = jnp.concatenate(pieces, 0)
        summed = jnp.einsum("kid,ke->eid", stacked.astype(jnp.float32), stacked_weight.astype(jnp.float32))
        hidden = jax.nn.relu(summed + pair_bias[:, None, None])
        return running + jnp.einsum("eid,e->id", hidden, head.astype(jnp.float32))

    running = lax.fori_loop(0, VIEWS, view_step, jnp.zeros((rows_out, BAND), jnp.float32))
    return running / VIEWS


def reference(bins, conv_weight, conv_bias, pair_left, pair_right, pair_weight, pair_bias, head, shifts, flags, dilations):
    total = bins.shape[0]
    kernels = view_kernels(conv_weight, flags)
    source = jnp.pad(bins, ((HALO, HALO), (0, 0)))
    left, right = trunk(source, HALO, total, shifts, dilations[0], kernels, conv_bias, pair_left, pair_right)
    left_pad = jnp.pad(left, ((0, 0), (DMAX, DMAX), (0, 0)))
    right_pad = jnp.pad(right, ((0, 0), (DMAX, DMAX + BAND), (0, 0)))

    def one_block(number):
        start = number * block_rows
        left_rows = lax.dynamic_slice_in_dim(left_pad, start, block_rows + 2 * DMAX, 1)
        right_rows = lax.dynamic_slice_in_dim(right_pad, start, block_rows + 2 * DMAX + BAND, 1)
        return pair_block(left_rows, right_rows, start - DMAX, total, dilations[1], pair_weight, pair_bias, head)

    blocks = lax.map(one_block, jnp.arange(total // block_rows, dtype=jnp.int32))
    return blocks.reshape(total, BAND)
```

```python
import functools

import jax
import jax.numpy as jnp
from jax import lax
from jax.experimental import pallas as pl
from jax.experimental.pallas import tpu as pltpu
from jax.sharding import PartitionSpec as P

BAND = 512
DMAX = 4
FIVE = 5
THREE = 3
TAPS = FIVE + 2
WIDE = 256
LANES = 128
LEAD = 16
NEAR = 48
HALO = 12
TILE = 16
CHUNKS = 3
FAR = -1e30
F32 = jnp.float32
BF16 = jnp.bfloat16
MESH = pl.DeviceIdType.MESH

SLOTS = sorted(
    [(k, b) for k in range(FIVE) for b in range(3)], key=lambda s: (s[0] + s[1], s[0])
) + sorted(
    [(k, b) for k in range(FIVE, TAPS) for b in range(3)], key=lambda s: (s[0] + s[1], s[0])
)


def row_groups(rows):
    tables = {}
    for r in range(1, DMAX + 1):
        fives, threes = [], []
        for first in range(min(r, rows)):
            size = -(-(rows - first) // r)
            best = None
            for a in range(size // FIVE + 2):
                b = max(0, -(-(size - FIVE * a) // THREE))
                cost = (FIVE * a + THREE * b != size, 4 * a + 3 * b)
                if best is None or cost < best[0]:
                    best = (cost, a, b)
            at = 0
            for _ in range(best[1]):
                fives.append(first + r * at)
                at += FIVE
            for _ in range(best[2]):
                threes.append(first + r * at)
                at += THREE
        tables[r] = (fives, threes)
    assert all(len(tables[r][n]) == len(tables[1][n]) for r in tables for n in range(2))
    return [list(zip(*[tables[r][n] for r in range(1, DMAX + 1)])) for n in range(2)]


def group_list(rows, r):
    result = []
    for n, size in enumerate((FIVE, THREE)):
        for starts in row_groups(rows)[n]:
            i0 = jnp.int32(starts[0])
            for value in range(2, DMAX + 1):
                i0 = jnp.where(r == value, starts[value - 1], i0)
            result.append((i0, size))
    return result


def dot(a, b, **kw):
    return jnp.dot(a, b, preferred_element_type=F32, **kw)


def dot_t(a, b):
    return lax.dot_general(a, b, (((0,), (0,)), ((), ())), preferred_element_type=F32)


def slot_of(index, size):
    total = jnp.zeros(index.shape, jnp.int32)
    for k in range(1, FIVE):
        total = total + (index >= k * size).astype(jnp.int32)
    return total


def lane_pick(tile, pc, key, load):
    lane = lax.broadcasted_iota(jnp.int32, (1, LANES), 1)
    first = tile * LANES // pc
    last = min((tile * LANES + LANES - 1) // pc, len(SLOTS) - 1)
    loaded = {}
    value, current = None, None
    for p in range(first, last + 1):
        want = key(SLOTS[p])
        if want == current:
            continue
        if want not in loaded:
            loaded[want] = load(want)
        value = loaded[want] if value is None else jnp.where(lane >= p * pc - tile * LANES, loaded[want], value)
        current = want
    return value


def sizes(rows, segments):
    total = rows * segments
    span = min(BAND + rows, total + TILE)
    chunk = -(-span // (CHUNKS * TILE)) * TILE
    blocks = -(-(rows + NEAR + HALO + CHUNKS * chunk) // rows)
    return total, span, chunk, blocks


def main_kernel(
    rows,
    segments,
    shifts,
    flags,
    dilations,
    x_ref,
    cw_ref,
    cb_ref,
    pleft_ref,
    pright_ref,
    pw_ref,
    pb_ref,
    head_ref,
    cols_ref,
    win,
    xf,
    kern,
    wall,
    lt,
    rt,
    lrows,
    ltile,
    band,
    hid,
    spread,
    send_sem,
    recv_sem,
    own_sem,
    ready,
):
    channels = win.shape[2]
    pc = pleft_ref.shape[0]
    views = shifts.shape[0]
    total, span, chunk, blocks = sizes(rows, segments)
    me = lax.axis_index("seg")
    base = me * rows
    reach = min(blocks - 2, segments - 1)
    q = dilations[0]
    r = dilations[1]
    tiles = wall.shape[0] // LANES

    barrier = pltpu.get_barrier_semaphore()
    for step in range(1, reach + 1):

        @pl.when(me + step < segments)
        def _():
            pl.semaphore_signal(barrier, inc=1, device_id={"seg": me + step}, device_id_type=MESH)

    own = pltpu.make_async_copy(x_ref, win.at[1], own_sem)
    own.start()

    @pl.when(me > 0)
    def _():
        pl.semaphore_wait(barrier, jnp.minimum(me, reach))
        pl.semaphore_signal(ready, inc=1, device_id={"seg": me - 1}, device_id_type=MESH)

    def copy(slot):
        return pltpu.make_async_remote_copy(
            src_ref=x_ref,
            dst_ref=win.at[slot],
            send_sem=send_sem.at[slot],
            recv_sem=recv_sem.at[slot],
            device_id={"seg": me - slot + 1},
            device_id_type=MESH,
        )

    for slot in reversed(range(2, reach + 2)):

        @pl.when(me - slot + 1 >= 0)
        def _():
            copy(slot).start()

    ci = lax.broadcasted_iota(jnp.int32, (channels, channels), 0)
    cj = lax.broadcasted_iota(jnp.int32, (channels, channels), 1)
    mirror = jnp.where(ci + cj == channels - 1, 1.0, 0.0).astype(BF16)
    for t in range(3):
        at = slice(t * channels, (t + 1) * channels)
        kern[0, at, :] = cw_ref[t]
        kern[1, at, :] = dot(mirror, cw_ref[2 - t]).astype(BF16)

    phases = rt.shape[1]
    lane = lax.broadcasted_iota(jnp.int32, (pc, phases * LANES), 1)
    chan = lax.broadcasted_iota(jnp.int32, (pc, phases * LANES), 0)
    repeat = jnp.zeros(lane.shape, F32)
    for k in range(phases * LANES // pc):
        repeat = jnp.where(lane - chan == k * pc, 1.0, repeat)
    wide_left = dot_t(pleft_ref[...], repeat.astype(BF16)).astype(BF16)
    wide_right = dot_t(pright_ref[...], repeat.astype(BF16)).astype(BF16)

    lane = lax.broadcasted_iota(jnp.int32, (pc, WIDE), 1)
    chan = lax.broadcasted_iota(jnp.int32, (pc, WIDE), 0)
    spots = [jnp.where(lane - chan == o * pc, 1.0, 0.0) for o in range(FIVE)]
    placed = [dot(pw_ref[...], spots[o].astype(BF16)) for o in range(FIVE)]
    for p, (k, b) in enumerate(SLOTS):
        block = None
        for o in range(FIVE):
            if 0 <= k - o <= 2:
                first = ((k - o) * 3 + b) * pc
                part = placed[o][first : first + pc]
                block = part if block is None else block + part
        wall[p * pc : (p + 1) * pc, :] = block.astype(BF16)
    used = len(SLOTS) * pc
    wall[used:, :] = jnp.zeros((wall.shape[0] - used, WIDE), BF16)

    bias8 = jnp.broadcast_to(pb_ref[...], (8, pc))
    bias = dot(bias8, sum(spots[1:], spots[0]), precision=lax.Precision.HIGHEST)[0:1, :]
    wi = lax.broadcasted_iota(jnp.int32, (WIDE, pc), 0)
    wc = lax.broadcasted_iota(jnp.int32, (WIDE, pc), 1)
    hit = wi == wc
    for o in range(1, FIVE):
        hit = hit | (wi - wc == o * pc)
    untile = jnp.where(hit, 1.0, 0.0).astype(BF16)
    head_b = jnp.broadcast_to(head_ref[...].astype(F32), (LANES, pc)).astype(BF16)
    head_rows = lax.dot_general(
        untile, head_b, (((1,), (1,)), ((), ())), preferred_element_type=F32
    )
    wide_row = lax.broadcasted_iota(jnp.int32, (WIDE, LANES), 0)
    target = lax.broadcasted_iota(jnp.int32, (WIDE, LANES), 1) - r * slot_of(wide_row, pc)
    groups = group_list(rows, r)
    for g, (i0, size) in enumerate(groups):
        mine = (target == i0) & (wide_row < size * pc)
        spread[g * WIDE : (g + 1) * WIDE, :] = jnp.where(mine, head_rows, 0.0).astype(BF16)
    empty = jnp.broadcast_to(jnp.maximum(bias, 0.0) * float(views), (TILE, WIDE)).astype(BF16)
    blank = dot(jnp.concatenate([empty] * len(groups), 1), spread[...])[0:8]
    rest = cols_ref.shape[0]
    cols_ref[...] = jnp.broadcast_to(blank[None], (rest // 8, 8, LANES)).reshape(rest, LANES)

    own.wait()

    @pl.when(me + 1 < segments)
    def _():
        pl.semaphore_wait(ready, 1)
        copy(0).start()

    def take(slot, _):
        source = me + slot - 1
        there = (source >= 0) & (source < segments)
        at = pl.ds(pl.multiple_of(slot * rows, rows), rows)

        @pl.when(there & (slot != 1))
        def _():
            copy(slot).wait_recv()

        @pl.when(there)
        def _():
            xf[at, :] = win[slot].astype(F32)

        @pl.when(jnp.logical_not(there))
        def _():
            xf[at, :] = jnp.zeros((rows, channels), F32)

        return 0

    def feature_of(v, first, count):
        start = rows + first + shifts[v]
        taps = [xf[pl.ds(start + (t - 1) * q, count), :] for t in range(3)]
        stacked = jnp.concatenate([t.astype(BF16) for t in taps], axis=1)
        mixed = dot(stacked, kern[flags[v]])
        return (taps[1] + jnp.maximum(mixed + cb_ref[...], 0.0)).astype(BF16)

    def inside(first, count):
        grow = lax.broadcasted_iota(jnp.int32, (count, 1), 0) + (base + first)
        return (grow >= 0) & (grow < total)

    def project(feature, wide, valid):
        value = dot(feature, wide).astype(BF16).astype(F32)
        return [
            jnp.where(valid, value[:, n * LANES : (n + 1) * LANES], FAR) for n in range(phases)
        ]

    near = LEAD + NEAR
    lax.fori_loop(0, 3, take, 0)
    valid = inside(-LEAD, near)
    for v in range(views):
        feature = feature_of(v, -LEAD, near)
        for n, part in enumerate(project(feature, wide_left, valid)):
            lt[v, n, :near, :] = part
            lt[v, n, near:, :] = jnp.full((lt.shape[2] - near, LANES), FAR, F32)
        for n, part in enumerate(project(feature, wide_right, valid)):
            rt[v, n, :near, :] = part
        for tile in range(tiles):
            lrows[v, tile] = lane_pick(
                tile,
                pc,
                lambda s: s[0] - 1,
                lambda k: lt[v, tile % phases, pl.ds(LEAD + k * r, rows), :],
            )
    for g, (i0, size) in enumerate(groups):
        for v in range(views):
            for tile in range(tiles):
                row = lrows[v, tile, pl.ds(i0, 1), :]
                ltile[g * views + v, :, tile * LANES : (tile + 1) * LANES] = jnp.broadcast_to(
                    row, (TILE, LANES)
                ).astype(BF16)

    def tap_lanes(b):
        lanes = lax.broadcasted_iota(jnp.int32, (1, wall.shape[0]), 1)
        value = jnp.zeros(lanes.shape, F32)
        for p, slot in enumerate(SLOTS):
            if slot[1] == b:
                value = jnp.where((lanes >= p * pc) & (lanes < (p + 1) * pc), 1.0, value)
        return value.astype(BF16)

    open_end = total > BAND
    edge = chunk if open_end else NEAR
    first_lanes = tap_lanes(0)
    last_lanes = tap_lanes(2)
    edge_row = lax.broadcasted_iota(jnp.int32, (edge, LANES), 0)

    def chunk_body(c, _):
        at = pl.multiple_of(c * chunk, TILE)
        low = jnp.where(c == 0, 3, (rows + NEAR + HALO + c * chunk + rows - 1) // rows)
        high = (rows + NEAR + HALO + (c + 1) * chunk + rows - 1) // rows
        lax.fori_loop(low, high, take, 0)
        valid = inside(NEAR + at, chunk)
        for v in range(views):
            feature = feature_of(v, NEAR + at, chunk)
            for n, part in enumerate(project(feature, wide_right, valid)):
                rt[v, n, pl.ds(pl.multiple_of(near + at, TILE), chunk), :] = part
            for tile in range(tiles):
                band[v, :, tile * LANES : (tile + 1) * LANES] = lane_pick(
                    tile,
                    pc,
                    lambda s: s[0] + s[1] - 2,
                    lambda s: rt[v, tile % phases, pl.ds(LEAD + at + s * r, chunk), :],
                ).astype(BF16)
        for g, (i0, size) in enumerate(groups):
            depth = WIDE * (4 if size == FIVE else 3)
            offset = edge_row + (at - i0)
            head_mask = jnp.where(offset < r, FAR, 0.0).astype(BF16)
            head_mask = jnp.concatenate([head_mask] * (depth // LANES), 1) * first_lanes[:, :depth]
            if open_end:
                tail = jnp.where(offset >= BAND - r, FAR, 0.0).astype(BF16)
                tail = jnp.concatenate([tail] * (depth // LANES), 1) * last_lanes[:, :depth]
                head_mask = head_mask + tail
            hidden = None
            for v in range(views):
                value = band[v, :, :depth].reshape(chunk // TILE, TILE, depth)
                value = (value + ltile[g * views + v, :, :depth][None]).reshape(chunk, depth)
                if open_end:
                    value = value + head_mask
                else:
                    value = jnp.concatenate([value[:edge] + head_mask, value[edge:]], 0)
                value = jnp.maximum(value, 0)
                term = jnp.maximum(dot(value, wall[:depth]) + bias, 0.0)
                hidden = term if hidden is None else hidden + term
            hid[:, g * WIDE : (g + 1) * WIDE] = hidden.astype(BF16)
        cols_ref[pl.ds(at, chunk), :] = dot(hid[...], spread[...])
        return 0

    count = (jnp.minimum(span, total + TILE - base) + chunk - 1) // chunk
    lax.fori_loop(0, count, chunk_body, 0)

    @pl.when(me + 1 < segments)
    def _():
        copy(0).wait_send()

    for slot in range(2, reach + 2):

        @pl.when(me - slot + 1 >= 0)
        def _():
            copy(slot).wait_send()


def place_kernel(rows, views, dilations, cols_ref, out_ref):
    r = dilations[1]
    lanes = cols_ref.shape[0]
    flat = cols_ref[...].T[:rows]
    row = lax.broadcasted_iota(jnp.int32, (rows, LANES), 0)
    moves = jnp.zeros((rows, LANES), jnp.int32)
    for i0, size in group_list(rows, r):
        for o in range(size):
            moves = jnp.where(row - i0 == o * r, i0, moves)
    moves = jnp.concatenate([moves] * (lanes // LANES), axis=1)
    bit = 1
    while bit < rows:
        flat = jnp.where((moves & bit) != 0, pltpu.roll(flat, lanes - bit, 1), flat)
        bit *= 2
    out_ref[...] = flat[:, :BAND] * (1.0 / views)


def per_device(
    bins,
    conv_weight,
    conv_bias,
    pair_left,
    pair_right,
    pair_weight,
    pair_bias,
    head,
    shifts,
    flags,
    dilations,
):
    rows, channels = bins.shape
    views = shifts.shape[0]
    pc = pair_left.shape[1]
    segments = lax.axis_size("seg")
    total, span, chunk, blocks = sizes(rows, segments)
    groups = sum(len(starts) for starts in row_groups(rows))
    depth = WIDE * 4
    lanes = -(-max(CHUNKS * chunk, BAND + rows) // LANES) * LANES
    filled = LEAD + NEAR + CHUNKS * chunk
    vmem = pl.BlockSpec(memory_space=pltpu.VMEM)
    smem = pl.BlockSpec(memory_space=pltpu.SMEM)
    cols = pl.pallas_call(
        functools.partial(main_kernel, rows, segments),
        out_shape=jax.ShapeDtypeStruct((lanes, LANES), F32),
        in_specs=[smem] * 3 + [pl.BlockSpec(memory_space=pl.ANY)] + [vmem] * 7,
        out_specs=vmem,
        scratch_shapes=[
            pltpu.VMEM((blocks, rows, channels), BF16),
            pltpu.VMEM((blocks * rows, channels), F32),
            pltpu.VMEM((2, 3 * channels, channels), BF16),
            pltpu.VMEM((depth, WIDE), BF16),
            pltpu.VMEM((views, 3, LEAD + NEAR + 16, LANES), F32),
            pltpu.VMEM((views, 3, filled, LANES), F32),
            pltpu.VMEM((views, depth // LANES, rows, LANES), F32),
            pltpu.VMEM((groups * views, TILE, depth), BF16),
            pltpu.VMEM((views, chunk, depth), BF16),
            pltpu.VMEM((chunk, groups * WIDE), BF16),
            pltpu.VMEM((groups * WIDE, LANES), BF16),
            pltpu.SemaphoreType.DMA((blocks,)),
            pltpu.SemaphoreType.DMA((blocks,)),
            pltpu.SemaphoreType.DMA,
            pltpu.SemaphoreType.REGULAR,
        ],
        compiler_params=pltpu.CompilerParams(
            collective_id=0, has_side_effects=True, vmem_limit_bytes=60 * 1024 * 1024
        ),
    )(
        shifts,
        flags,
        dilations,
        bins,
        conv_weight,
        conv_bias.reshape(1, channels),
        pair_left.T,
        pair_right.T,
        pair_weight.reshape(9 * pc, pc),
        pair_bias.reshape(1, pc),
        head.reshape(1, pc),
    )
    return pl.pallas_call(
        functools.partial(place_kernel, rows, views),
        out_shape=jax.ShapeDtypeStruct((rows, BAND), F32),
        in_specs=[smem, vmem],
        out_specs=vmem,
    )(dilations, cols)


def solution(mesh):
    placed = (P(("groups", "seg"), None), P(), P(), P(), P(), P(), P(), P(), P(), P(), P())
    return jax.shard_map(
        per_device,
        mesh=mesh,
        in_specs=placed,
        out_specs=P(("groups", "seg"), None),
        check_vma=False,
    )
```

```python
import functools

import jax
import jax.numpy as jnp
from jax import lax
from jax.experimental import pallas as pl
from jax.experimental.pallas import tpu as pltpu
from jax.sharding import PartitionSpec as P

BAND = 512
DMAX = 4
FIVE = 5
THREE = 3
TAPS = FIVE + 2
WIDE = 256
LANES = 128
LEAD = 16
NEAR = 48
HALO = DMAX
TILE = 16
CHUNKS = 3
FAR = -1e30
F32 = jnp.float32
BF16 = jnp.bfloat16
MESH = pl.DeviceIdType.MESH

SLOTS = sorted(
    [(k, b) for k in range(FIVE) for b in range(3)], key=lambda s: (s[0] + s[1], s[0])
) + sorted(
    [(k, b) for k in range(FIVE, TAPS) for b in range(3)], key=lambda s: (s[0] + s[1], s[0])
)


def row_groups(rows):
    tables = {}
    for r in range(1, DMAX + 1):
        fives, threes = [], []
        for first in range(min(r, rows)):
            size = -(-(rows - first) // r)
            best = None
            for a in range(size // FIVE + 2):
                b = max(0, -(-(size - FIVE * a) // THREE))
                cost = (FIVE * a + THREE * b != size, 4 * a + 3 * b)
                if best is None or cost < best[0]:
                    best = (cost, a, b)
            at = 0
            for _ in range(best[1]):
                fives.append(first + r * at)
                at += FIVE
            for _ in range(best[2]):
                threes.append(first + r * at)
                at += THREE
        tables[r] = (fives, threes)
    assert all(len(tables[r][n]) == len(tables[1][n]) for r in tables for n in range(2))
    return [list(zip(*[tables[r][n] for r in range(1, DMAX + 1)])) for n in range(2)]


def group_list(rows, r):
    result = []
    for n, size in enumerate((FIVE, THREE)):
        for starts in row_groups(rows)[n]:
            i0 = jnp.int32(starts[0])
            for value in range(2, DMAX + 1):
                i0 = jnp.where(r == value, starts[value - 1], i0)
            result.append((i0, size))
    return result


def dot(a, b, **kw):
    return jnp.dot(a, b, preferred_element_type=F32, **kw)


def dot_t(a, b):
    return lax.dot_general(a, b, (((0,), (0,)), ((), ())), preferred_element_type=F32)


def slot_of(index, size):
    total = jnp.zeros(index.shape, jnp.int32)
    for k in range(1, FIVE):
        total = total + (index >= k * size).astype(jnp.int32)
    return total


def lane_pick(tile, pc, key, load):
    lane = lax.broadcasted_iota(jnp.int32, (1, LANES), 1)
    first = tile * LANES // pc
    last = min((tile * LANES + LANES - 1) // pc, len(SLOTS) - 1)
    loaded = {}
    value, current = None, None
    for p in range(first, last + 1):
        want = key(SLOTS[p])
        if want == current:
            continue
        if want not in loaded:
            loaded[want] = load(want)
        value = loaded[want] if value is None else jnp.where(lane >= p * pc - tile * LANES, loaded[want], value)
        current = want
    return value


def sizes(rows, segments):
    total = rows * segments
    span = min(BAND + rows, total + TILE)
    chunk = -(-span // (CHUNKS * TILE)) * TILE
    blocks = -(-(rows + NEAR + HALO + CHUNKS * chunk) // rows)
    return total, span, chunk, blocks


def main_kernel(
    rows,
    segments,
    shifts,
    flags,
    dilations,
    x_ref,
    cw_ref,
    cb_ref,
    pleft_ref,
    pright_ref,
    pw_ref,
    pb_ref,
    head_ref,
    cols_ref,
    win,
    xf,
    kern,
    wide,
    wall,
    lt,
    rt,
    lrows,
    ltile,
    band,
    hid,
    spread,
    send_sem,
    recv_sem,
    own_sem,
    ready,
):
    channels = win.shape[2]
    pc = pleft_ref.shape[0]
    views = shifts.shape[0]
    total, span, chunk, blocks = sizes(rows, segments)
    me = lax.axis_index("seg")
    base = me * rows
    reach = min(blocks - 2, segments - 1)
    q = dilations[0]
    r = dilations[1]
    tiles = wall.shape[0] // LANES

    barrier = pltpu.get_barrier_semaphore()
    for step in range(1, reach + 1):

        @pl.when(me + step < segments)
        def _():
            pl.semaphore_signal(barrier, inc=1, device_id={"seg": me + step}, device_id_type=MESH)

    own = pltpu.make_async_copy(x_ref, win.at[1], own_sem)
    own.start()
    own.wait()

    @pl.when(me > 0)
    def _():
        pl.semaphore_wait(barrier, jnp.minimum(me, reach))
        pl.semaphore_signal(ready, inc=1, device_id={"seg": me - 1}, device_id_type=MESH)

    def copy(slot):
        return pltpu.make_async_remote_copy(
            src_ref=win.at[1],
            dst_ref=win.at[slot],
            send_sem=send_sem.at[slot],
            recv_sem=recv_sem.at[slot],
            device_id={"seg": me - slot + 1},
            device_id_type=MESH,
        )

    for slot in reversed(range(2, reach + 2)):

        @pl.when(me - slot + 1 >= 0)
        def _():
            copy(slot).start()

    ci = lax.broadcasted_iota(jnp.int32, (channels, channels), 0)
    cj = lax.broadcasted_iota(jnp.int32, (channels, channels), 1)
    mirror = jnp.where(ci + cj == channels - 1, 1.0, 0.0).astype(BF16)
    for t in range(3):
        at = slice(t * channels, (t + 1) * channels)
        kern[at, :channels] = cw_ref[t]
        kern[at, channels:] = dot(mirror, cw_ref[2 - t]).astype(BF16)

    phases = rt.shape[1]
    lane = lax.broadcasted_iota(jnp.int32, (pc, phases * LANES), 1)
    chan = lax.broadcasted_iota(jnp.int32, (pc, phases * LANES), 0)
    repeat = jnp.zeros(lane.shape, F32)
    for k in range(phases * LANES // pc):
        repeat = jnp.where(lane - chan == k * pc, 1.0, repeat)
    repeat = repeat.astype(BF16)
    across = phases * LANES
    for n, side in enumerate((pleft_ref, pright_ref)):
        part = dot_t(side[...], repeat).astype(BF16)
        for f in range(2):
            for h in range(2):
                wide[n, f * channels : (f + 1) * channels, h * across : (h + 1) * across] = (
                    part if f == h else jnp.zeros_like(part)
                )

    lane = lax.broadcasted_iota(jnp.int32, (pc, WIDE), 1)
    chan = lax.broadcasted_iota(jnp.int32, (pc, WIDE), 0)
    spots = [jnp.where(lane - chan == o * pc, 1.0, 0.0) for o in range(FIVE)]
    placed = [dot(pw_ref[...], spots[o].astype(BF16)) for o in range(FIVE)]
    for p, (k, b) in enumerate(SLOTS):
        block = None
        for o in range(FIVE):
            if 0 <= k - o <= 2:
                first = ((k - o) * 3 + b) * pc
                part = placed[o][first : first + pc]
                block = part if block is None else block + part
        wall[p * pc : (p + 1) * pc, :] = block.astype(BF16)
    used = len(SLOTS) * pc
    wall[used:, :] = jnp.zeros((wall.shape[0] - used, WIDE), BF16)

    bias8 = jnp.broadcast_to(pb_ref[...], (8, pc))
    bias = dot(bias8, sum(spots[1:], spots[0]), precision=lax.Precision.HIGHEST)[0:1, :]
    wi = lax.broadcasted_iota(jnp.int32, (WIDE, pc), 0)
    wc = lax.broadcasted_iota(jnp.int32, (WIDE, pc), 1)
    hit = wi == wc
    for o in range(1, FIVE):
        hit = hit | (wi - wc == o * pc)
    untile = jnp.where(hit, 1.0, 0.0).astype(BF16)
    head_b = jnp.broadcast_to(head_ref[...].astype(F32), (LANES, pc)).astype(BF16)
    head_rows = lax.dot_general(
        untile, head_b, (((1,), (1,)), ((), ())), preferred_element_type=F32
    )
    wide_row = lax.broadcasted_iota(jnp.int32, (WIDE, LANES), 0)
    target = lax.broadcasted_iota(jnp.int32, (WIDE, LANES), 1) - r * slot_of(wide_row, pc)
    groups = group_list(rows, r)
    for g, (i0, size) in enumerate(groups):
        mine = (target == i0) & (wide_row < size * pc)
        spread[g * WIDE : (g + 1) * WIDE, :] = jnp.where(mine, head_rows, 0.0).astype(BF16)
    empty = jnp.broadcast_to(jnp.maximum(bias, 0.0) * float(views), (TILE, WIDE)).astype(BF16)
    blank = dot(jnp.concatenate([empty] * len(groups), 1), spread[...])[0:8]
    rest = cols_ref.shape[0]
    cols_ref[...] = jnp.broadcast_to(blank[None], (rest // 8, 8, LANES)).reshape(rest, LANES)

    @pl.when(me + 1 < segments)
    def _():
        pl.semaphore_wait(ready, 1)
        copy(0).start()

    def take(slot, _):
        source = me + slot - 1
        there = (source >= 0) & (source < segments)
        at = pl.ds(pl.multiple_of(slot * rows, rows), rows)

        @pl.when(there & (slot != 1))
        def _():
            copy(slot).wait_recv()

        @pl.when(there)
        def _():
            xf[at, :] = win[slot].astype(F32)

        @pl.when(jnp.logical_not(there))
        def _():
            xf[at, :] = jnp.zeros((rows, channels), F32)

        return 0

    trunk_bias = jnp.concatenate([cb_ref[...]] * 2, 1)

    def project(out, side, first, at, count):
        taps = [xf[pl.ds(rows + first + (t - 1) * q, count), :] for t in range(3)]
        stacked = jnp.concatenate([t.astype(BF16) for t in taps], axis=1)
        mixed = dot(stacked, kern[...])
        center = jnp.concatenate([taps[1]] * 2, 1)
        feature = (center + jnp.maximum(mixed + trunk_bias, 0.0)).astype(BF16)
        for n in side:
            value = dot(feature, wide[n])
            for f in range(2):
                for p in range(phases):
                    part = (f * phases + p) * LANES
                    out[n][f, p, pl.ds(at, count), :] = value[:, part : part + LANES]

    near = LEAD + NEAR
    lax.fori_loop(0, 3, take, 0)
    project((lt, rt), (0, 1), -LEAD, 0, near)
    lt[:, :, near:, :] = jnp.zeros((2, phases, lt.shape[2] - near, LANES), F32)
    left_row = lax.broadcasted_iota(jnp.int32, (rows, LANES), 0) + base
    for v in range(views):
        for tile in range(tiles):

            def left_at(k):
                value = lt[flags[v], tile % phases, pl.ds(LEAD + k * r + shifts[v], rows), :]
                row = left_row + k * r
                return jnp.where((row >= 0) & (row < total), value, FAR)

            lrows[v, tile] = lane_pick(tile, pc, lambda s: s[0] - 1, left_at)
    for g, (i0, size) in enumerate(groups):
        for v in range(views):
            for tile in range(tiles):
                row = lrows[v, tile, pl.ds(i0, 1), :]
                ltile[g * views + v, :, tile * LANES : (tile + 1) * LANES] = jnp.broadcast_to(
                    row, (TILE, LANES)
                ).astype(BF16)

    def tap_lanes(b):
        lanes = lax.broadcasted_iota(jnp.int32, (1, wall.shape[0]), 1)
        value = jnp.zeros(lanes.shape, F32)
        for p, slot in enumerate(SLOTS):
            if slot[1] == b:
                value = jnp.where((lanes >= p * pc) & (lanes < (p + 1) * pc), 1.0, value)
        return value.astype(BF16)

    open_end = total > BAND
    edge = chunk if open_end else NEAR
    first_lanes = tap_lanes(0)
    last_lanes = tap_lanes(2)
    middle = chunk // TILE // 2 * TILE
    pieces = ((0, middle), (middle, chunk))

    def chunk_body(c, _):
        at = pl.multiple_of(c * chunk, TILE)
        low = jnp.where(c == 0, 3, (rows + NEAR + HALO + c * chunk + rows - 1) // rows)
        high = (rows + NEAR + HALO + (c + 1) * chunk + rows - 1) // rows
        lax.fori_loop(low, high, take, 0)
        project((lt, rt), (1,), NEAR + at, pl.multiple_of(near + at, TILE), chunk)
        for lo, hi in pieces:
            size_m = hi - lo
            column = lax.broadcasted_iota(jnp.int32, (size_m, LANES), 0) + (at + lo + base)
            for tile in range(tiles):
                reach_m = lane_pick(tile, pc, lambda s: s[0] + s[1] - 2, lambda s: total - s * r)
                known = column < reach_m
                for v in range(views):
                    value = lane_pick(
                        tile,
                        pc,
                        lambda s: s[0] + s[1] - 2,
                        lambda s: rt[
                            flags[v],
                            tile % phases,
                            pl.ds(LEAD + at + lo + s * r + shifts[v], size_m),
                            :,
                        ],
                    )
                    band[v, lo:hi, tile * LANES : (tile + 1) * LANES] = jnp.where(
                        known, value, FAR
                    ).astype(BF16)
            for g, (i0, size) in enumerate(groups):
                depth = WIDE * (4 if size == FIVE else 3)
                masks = None
                if lo < edge:
                    end = min(hi, edge) - lo
                    offset = lax.broadcasted_iota(jnp.int32, (end, LANES), 0) + (at + lo - i0)
                    masks = jnp.where(offset < r, FAR, 0.0).astype(BF16)
                    masks = jnp.concatenate([masks] * (depth // LANES), 1) * first_lanes[:, :depth]
                    if open_end:
                        tail = jnp.where(offset >= BAND - r, FAR, 0.0).astype(BF16)
                        tail = jnp.concatenate([tail] * (depth // LANES), 1)
                        masks = masks + tail * last_lanes[:, :depth]
                values = []
                for v in range(views):
                    value = band[v, lo:hi, :depth].reshape(size_m // TILE, TILE, depth)
                    value = value + ltile[g * views + v, :, :depth][None]
                    value = value.reshape(size_m, depth)
                    if masks is not None:
                        parts = [value[:end] + masks]
                        if end < size_m:
                            parts.append(value[end:])
                        value = jnp.concatenate(parts, 0)
                    values.append(jnp.maximum(value, 0))
                term = jnp.maximum(dot(jnp.concatenate(values, 0), wall[:depth]) + bias, 0.0)
                hidden = term[:size_m]
                for v in range(1, views):
                    hidden = hidden + term[v * size_m : (v + 1) * size_m]
                hid[lo:hi, g * WIDE : (g + 1) * WIDE] = hidden.astype(BF16)
        cols_ref[pl.ds(at, chunk), :] = dot(hid[...], spread[...])
        return 0

    count = (jnp.minimum(span, total + TILE - base) + chunk - 1) // chunk
    lax.fori_loop(0, count, chunk_body, 0)

    @pl.when(me + 1 < segments)
    def _():
        copy(0).wait_send()

    for slot in range(2, reach + 2):

        @pl.when(me - slot + 1 >= 0)
        def _():
            copy(slot).wait_send()


def place_kernel(rows, views, dilations, cols_ref, out_ref):
    r = dilations[1]
    lanes = cols_ref.shape[0]
    flat = cols_ref[...].T[:rows]
    row = lax.broadcasted_iota(jnp.int32, (rows, LANES), 0)
    moves = jnp.zeros((rows, LANES), jnp.int32)
    for i0, size in group_list(rows, r):
        for o in range(size):
            moves = jnp.where(row - i0 == o * r, i0, moves)
    moves = jnp.concatenate([moves] * (lanes // LANES), axis=1)
    bit = 1
    while bit < rows:
        flat = jnp.where((moves & bit) != 0, pltpu.roll(flat, lanes - bit, 1), flat)
        bit *= 2
    out_ref[...] = flat[:, :BAND] * (1.0 / views)


def per_device(
    bins,
    conv_weight,
    conv_bias,
    pair_left,
    pair_right,
    pair_weight,
    pair_bias,
    head,
    shifts,
    flags,
    dilations,
):
    rows, channels = bins.shape
    views = shifts.shape[0]
    pc = pair_left.shape[1]
    segments = lax.axis_size("seg")
    total, span, chunk, blocks = sizes(rows, segments)
    groups = sum(len(starts) for starts in row_groups(rows))
    depth = WIDE * 4
    lanes = -(-max(CHUNKS * chunk, BAND + rows) // LANES) * LANES
    filled = LEAD + NEAR + CHUNKS * chunk
    vmem = pl.BlockSpec(memory_space=pltpu.VMEM)
    smem = pl.BlockSpec(memory_space=pltpu.SMEM)
    cols = pl.pallas_call(
        functools.partial(main_kernel, rows, segments),
        out_shape=jax.ShapeDtypeStruct((lanes, LANES), F32),
        in_specs=[smem] * 3 + [pl.BlockSpec(memory_space=pl.ANY)] + [vmem] * 7,
        out_specs=vmem,
        scratch_shapes=[
            pltpu.VMEM((blocks, rows, channels), BF16),
            pltpu.VMEM((blocks * rows, channels), F32),
            pltpu.VMEM((3 * channels, 2 * channels), BF16),
            pltpu.VMEM((2, 2 * channels, 2 * 3 * LANES), BF16),
            pltpu.VMEM((depth, WIDE), BF16),
            pltpu.VMEM((2, 3, LEAD + NEAR + 16, LANES), F32),
            pltpu.VMEM((2, 3, filled, LANES), F32),
            pltpu.VMEM((views, depth // LANES, rows, LANES), F32),
            pltpu.VMEM((groups * views, TILE, depth), BF16),
            pltpu.VMEM((views, chunk, depth), BF16),
            pltpu.VMEM((chunk, groups * WIDE), BF16),
            pltpu.VMEM((groups * WIDE, LANES), BF16),
            pltpu.SemaphoreType.DMA((blocks,)),
            pltpu.SemaphoreType.DMA((blocks,)),
            pltpu.SemaphoreType.DMA,
            pltpu.SemaphoreType.REGULAR,
        ],
        compiler_params=pltpu.CompilerParams(
            collective_id=0, has_side_effects=True, vmem_limit_bytes=60 * 1024 * 1024
        ),
    )(
        shifts,
        flags,
        dilations,
        bins,
        conv_weight,
        conv_bias.reshape(1, channels),
        pair_left.T,
        pair_right.T,
        pair_weight.reshape(9 * pc, pc),
        pair_bias.reshape(1, pc),
        head.reshape(1, pc),
    )
    return pl.pallas_call(
        functools.partial(place_kernel, rows, views),
        out_shape=jax.ShapeDtypeStruct((rows, BAND), F32),
        in_specs=[smem, vmem],
        out_specs=vmem,
    )(dilations, cols)


def solution(mesh):
    placed = (P(("groups", "seg"), None), P(), P(), P(), P(), P(), P(), P(), P(), P(), P())
    return jax.shard_map(
        per_device,
        mesh=mesh,
        in_specs=placed,
        out_specs=P(("groups", "seg"), None),
        check_vma=False,
    )
```

```python
import functools

import jax
import jax.numpy as jnp
from jax import lax
from jax.experimental import pallas as pl
from jax.experimental.pallas import tpu as pltpu
from jax.sharding import PartitionSpec as P

BAND = 512
DMAX = 4
FIVE = 5
THREE = 3
TAPS = FIVE + 2
WIDE = 256
LANES = 128
LEAD = 16
NEAR = 48
HALO = DMAX
TILE = 16
CHUNK = 208
PIECE = 144
FRONT = 32
FAR = -1e30
F32 = jnp.float32
BF16 = jnp.bfloat16
MESH = pl.DeviceIdType.MESH

SLOTS = sorted(
    [(k, b) for k in range(FIVE) for b in range(3)], key=lambda s: (s[0] + s[1], s[0])
) + sorted(
    [(k, b) for k in range(FIVE, TAPS) for b in range(3)], key=lambda s: (s[0] + s[1], s[0])
)


def row_groups(rows):
    tables = {}
    for r in range(1, DMAX + 1):
        fives, threes = [], []
        for first in range(min(r, rows)):
            size = -(-(rows - first) // r)
            best = None
            for a in range(size // FIVE + 2):
                b = max(0, -(-(size - FIVE * a) // THREE))
                cost = (FIVE * a + THREE * b != size, 4 * a + 3 * b)
                if best is None or cost < best[0]:
                    best = (cost, a, b)
            at = 0
            for _ in range(best[1]):
                fives.append(first + r * at)
                at += FIVE
            for _ in range(best[2]):
                threes.append(first + r * at)
                at += THREE
        tables[r] = (fives, threes)
    assert all(len(tables[r][n]) == len(tables[1][n]) for r in tables for n in range(2))
    return [list(zip(*[tables[r][n] for r in range(1, DMAX + 1)])) for n in range(2)]


def group_list(rows, r):
    result = []
    for n, size in enumerate((FIVE, THREE)):
        for starts in row_groups(rows)[n]:
            i0 = jnp.int32(starts[0])
            for value in range(2, DMAX + 1):
                i0 = jnp.where(r == value, starts[value - 1], i0)
            result.append((i0, size))
    return result


def dot(a, b, **kw):
    return jnp.dot(a, b, preferred_element_type=F32, **kw)


def dot_t(a, b):
    return lax.dot_general(a, b, (((0,), (0,)), ((), ())), preferred_element_type=F32)


def slot_of(index, size):
    total = jnp.zeros(index.shape, jnp.int32)
    for k in range(1, FIVE):
        total = total + (index >= k * size).astype(jnp.int32)
    return total


def lane_pick(tile, pc, key, load):
    lane = lax.broadcasted_iota(jnp.int32, (1, LANES), 1)
    first = tile * LANES // pc
    last = min((tile * LANES + LANES - 1) // pc, len(SLOTS) - 1)
    loaded = {}
    value, current = None, None
    for p in range(first, last + 1):
        want = key(SLOTS[p])
        if want == current:
            continue
        if want not in loaded:
            loaded[want] = load(want)
        value = loaded[want] if value is None else jnp.where(lane >= p * pc - tile * LANES, loaded[want], value)
        current = want
    return value


def sizes(rows, segments):
    total = rows * segments
    span = min(BAND + rows, total + TILE)
    chunks = -(-span // CHUNK)
    owners = -(-(total + TILE - 2 * CHUNK) // rows)
    far = (segments - owners) * rows
    helped = (
        total <= BAND
        and 0 < owners
        and 2 * owners <= segments - owners
        and far <= 2 * CHUNK
        and span <= far + PIECE
        and total + TILE - far <= PIECE
    )
    if helped:
        chunks = 2
    else:
        owners = 0
    blocks = -(-(rows + FRONT + HALO + chunks * CHUNK) // rows)
    return total, span, chunks, owners, blocks


def main_kernel(
    rows,
    segments,
    shifts,
    flags,
    dilations,
    x_ref,
    cw_ref,
    cb_ref,
    pleft_ref,
    pright_ref,
    pw_ref,
    pb_ref,
    head_ref,
    out_ref,
    win,
    xf,
    kern,
    wide,
    wall,
    lt,
    rt,
    lrows,
    ltile,
    band,
    hid,
    spread,
    cols,
    upright,
    owner_win,
    owner_xf,
    back,
    far,
    send_sem,
    recv_sem,
    own_sem,
    ready,
    up_send,
    up_recv,
    up_ready,
    back_send,
    back_recv,
):
    channels = win.shape[2]
    pc = pleft_ref.shape[0]
    views = shifts.shape[0]
    total, span, chunks, owners, blocks = sizes(rows, segments)
    chunk = CHUNK
    lift = segments - owners
    me = lax.axis_index("seg")
    base = me * rows
    reach = min(blocks - 2, segments - 1)
    q = dilations[0]
    r = dilations[1]
    tiles = wall.shape[0] // LANES

    barrier = pltpu.get_barrier_semaphore()
    for step in range(1, reach + 1):

        @pl.when(me + step < segments)
        def _():
            pl.semaphore_signal(barrier, inc=1, device_id={"seg": me + step}, device_id_type=MESH)

    own = pltpu.make_async_copy(x_ref, win.at[1], own_sem)
    own.start()
    own.wait()

    @pl.when(me > 0)
    def _():
        pl.semaphore_wait(barrier, jnp.minimum(me, reach))
        pl.semaphore_signal(ready, inc=1, device_id={"seg": me - 1}, device_id_type=MESH)

    def copy_up(k):
        return pltpu.make_async_remote_copy(
            src_ref=win.at[1],
            dst_ref=owner_win.at[k],
            send_sem=up_send.at[k],
            recv_sem=up_recv.at[k],
            device_id={"seg": me - k + 1 + lift},
            device_id_type=MESH,
        )

    def copy_back():
        return pltpu.make_async_remote_copy(
            src_ref=back,
            dst_ref=far,
            send_sem=back_send,
            recv_sem=back_recv,
            device_id={"seg": me - lift},
            device_id_type=MESH,
        )

    helper = (me >= lift) if owners else None
    for k in range(3 if owners else 0):
        other = me - lift + k - 1

        @pl.when(helper & (other >= 0))
        def _():
            pl.semaphore_signal(up_ready.at[k], inc=1, device_id={"seg": other}, device_id_type=MESH)

    def lifts(k):
        return (me - k + 1 >= 0) & (me - k + 1 < owners)

    def copy(slot):
        return pltpu.make_async_remote_copy(
            src_ref=win.at[1],
            dst_ref=win.at[slot],
            send_sem=send_sem.at[slot],
            recv_sem=recv_sem.at[slot],
            device_id={"seg": me - slot + 1},
            device_id_type=MESH,
        )

    first_slots = -(-(rows + FRONT + HALO + chunk) // rows)
    order = [slot for slot in reversed(range(2, reach + 2)) if slot < first_slots]
    order += [slot for slot in reversed(range(2, reach + 2)) if slot >= first_slots]
    for slot in order:

        @pl.when(me - slot + 1 >= 0)
        def _():
            copy(slot).start()

    ci = lax.broadcasted_iota(jnp.int32, (channels, channels), 0)
    cj = lax.broadcasted_iota(jnp.int32, (channels, channels), 1)
    mirror = jnp.where(ci + cj == channels - 1, 1.0, 0.0).astype(BF16)
    for t in range(3):
        at = slice(t * channels, (t + 1) * channels)
        kern[at, :channels] = cw_ref[t]
        kern[at, channels:] = dot(mirror, cw_ref[2 - t]).astype(BF16)

    phases = rt.shape[1]
    lane = lax.broadcasted_iota(jnp.int32, (pc, phases * LANES), 1)
    chan = lax.broadcasted_iota(jnp.int32, (pc, phases * LANES), 0)
    repeat = jnp.zeros(lane.shape, F32)
    for k in range(phases * LANES // pc):
        repeat = jnp.where(lane - chan == k * pc, 1.0, repeat)
    repeat = repeat.astype(BF16)
    across = phases * LANES
    for n, side in enumerate((pleft_ref, pright_ref)):
        part = dot_t(side[...], repeat).astype(BF16)
        for f in range(2):
            for h in range(2):
                wide[n, f * channels : (f + 1) * channels, h * across : (h + 1) * across] = (
                    part if f == h else jnp.zeros_like(part)
                )

    lane = lax.broadcasted_iota(jnp.int32, (pc, WIDE), 1)
    chan = lax.broadcasted_iota(jnp.int32, (pc, WIDE), 0)
    spots = [jnp.where(lane - chan == o * pc, 1.0, 0.0) for o in range(FIVE)]
    placed = [dot(pw_ref[...], spots[o].astype(BF16)) for o in range(FIVE)]
    for p, (k, b) in enumerate(SLOTS):
        block = None
        for o in range(FIVE):
            if 0 <= k - o <= 2:
                first = ((k - o) * 3 + b) * pc
                part = placed[o][first : first + pc]
                block = part if block is None else block + part
        wall[p * pc : (p + 1) * pc, :] = block.astype(BF16)
    used = len(SLOTS) * pc
    wall[used:, :] = jnp.zeros((wall.shape[0] - used, WIDE), BF16)

    bias8 = jnp.broadcast_to(pb_ref[...], (8, pc))
    bias = dot(bias8, sum(spots[1:], spots[0]), precision=lax.Precision.HIGHEST)[0:1, :]
    wi = lax.broadcasted_iota(jnp.int32, (WIDE, pc), 0)
    wc = lax.broadcasted_iota(jnp.int32, (WIDE, pc), 1)
    hit = wi == wc
    for o in range(1, FIVE):
        hit = hit | (wi - wc == o * pc)
    untile = jnp.where(hit, 1.0, 0.0).astype(BF16)
    head_b = jnp.broadcast_to(head_ref[...].astype(F32), (LANES, pc)).astype(BF16)
    head_rows = lax.dot_general(
        untile, head_b, (((1,), (1,)), ((), ())), preferred_element_type=F32
    )
    wide_row = lax.broadcasted_iota(jnp.int32, (WIDE, LANES), 0)
    target = lax.broadcasted_iota(jnp.int32, (WIDE, LANES), 1) - r * slot_of(wide_row, pc)
    groups = group_list(rows, r)
    for g, (i0, size) in enumerate(groups):
        mine = (target == i0) & (wide_row < size * pc)
        spread[g * WIDE : (g + 1) * WIDE, :] = jnp.where(mine, head_rows, 0.0).astype(BF16)
    empty = jnp.broadcast_to(jnp.maximum(bias, 0.0) * float(views), (TILE, WIDE)).astype(BF16)
    blank = dot(jnp.concatenate([empty] * len(groups), 1), spread[...])[0:8]
    rest = cols.shape[0]
    cols[...] = jnp.broadcast_to(blank[None], (rest // 8, 8, LANES)).reshape(rest, LANES)

    @pl.when(me + 1 < segments)
    def _():
        pl.semaphore_wait(ready, 1)
        copy(0).start()

    def take(slot, _):
        source = me + slot - 1
        there = (source >= 0) & (source < segments)
        at = pl.ds(pl.multiple_of(slot * rows, rows), rows)

        @pl.when(there & (slot != 1))
        def _():
            copy(slot).wait_recv()

        @pl.when(there)
        def _():
            xf[at, :] = win[slot].astype(F32)

        @pl.when(jnp.logical_not(there))
        def _():
            xf[at, :] = jnp.zeros((rows, channels), F32)

        return 0

    trunk_bias = jnp.concatenate([cb_ref[...]] * 2, 1)

    def project(source, out, side, first, at, count):
        taps = [source[pl.ds(rows + first + (t - 1) * q, count), :] for t in range(3)]
        stacked = jnp.concatenate([t.astype(BF16) for t in taps], axis=1)
        mixed = dot(stacked, kern[...])
        center = jnp.concatenate([taps[1]] * 2, 1)
        feature = (center + jnp.maximum(mixed + trunk_bias, 0.0)).astype(BF16)
        for n in side:
            value = dot(feature, wide[n])
            for f in range(2):
                for p in range(phases):
                    part = (f * phases + p) * LANES
                    out[n][f, p, pl.ds(at, count), :] = value[:, part : part + LANES]

    def send_up(now):
        for k in range(3 if owners else 0):

            @pl.when(lifts(k) & now)
            def _():
                pl.semaphore_wait(up_ready.at[k], 1)
                copy_up(k).start()

    send_up(me >= 2)
    near = LEAD + NEAR
    lax.fori_loop(0, 3, take, 0)
    project(xf, (lt.at[0], rt), (0, 1), -LEAD, 0, near)
    lt[:, :, :, near:, :] = jnp.zeros((2, 2, phases, lt.shape[3] - near, LANES), F32)

    def left_tiles(which, first):
        left_row = lax.broadcasted_iota(jnp.int32, (rows, LANES), 0) + first
        for v in range(views):
            for tile in range(tiles):

                def left_at(k):
                    value = lt[which, flags[v], tile % phases, pl.ds(LEAD + k * r + shifts[v], rows), :]
                    row = left_row + k * r
                    return jnp.where((row >= 0) & (row < total), value, FAR)

                lrows[v, tile] = lane_pick(tile, pc, lambda s: s[0] - 1, left_at)
        for g, (i0, size) in enumerate(groups):
            for v in range(views):
                for tile in range(tiles):
                    row = lrows[v, tile, pl.ds(i0, 1), :]
                    ltile[g * views + v, :, tile * LANES : (tile + 1) * LANES] = (
                        jnp.broadcast_to(row, (TILE, LANES)).astype(BF16)
                    )

    send_up(me < 2)

    def tap_lanes(b):
        lanes = lax.broadcasted_iota(jnp.int32, (1, wall.shape[0]), 1)
        value = jnp.zeros(lanes.shape, F32)
        for p, slot in enumerate(SLOTS):
            if slot[1] == b:
                value = jnp.where((lanes >= p * pc) & (lanes < (p + 1) * pc), 1.0, value)
        return value.astype(BF16)

    open_end = total > BAND
    edge = chunk if open_end else NEAR
    first_lanes = tap_lanes(0)
    last_lanes = tap_lanes(2)
    pieces = ((0, PIECE), (PIECE, chunk))

    def fill(at, lo, hi):
        size_m = hi - lo
        column = lax.broadcasted_iota(jnp.int32, (size_m, LANES), 0) + (at + lo + base)
        for tile in range(tiles):
            reach_m = lane_pick(tile, pc, lambda s: s[0] + s[1] - 2, lambda s: total - s * r)
            known = column < reach_m
            for v in range(views):
                value = lane_pick(
                    tile,
                    pc,
                    lambda s: s[0] + s[1] - 2,
                    lambda s: rt[
                        flags[v],
                        tile % phases,
                        pl.ds(LEAD + at + lo + s * r + shifts[v], size_m),
                        :,
                    ],
                )
                band[v, lo:hi, tile * LANES : (tile + 1) * LANES] = jnp.where(
                    known, value, FAR
                ).astype(BF16)

    def build(c, at):
        low = jnp.where(c == 0, 3, (rows + FRONT + HALO + c * chunk + rows - 1) // rows)
        high = (rows + FRONT + HALO + (c + 1) * chunk + rows - 1) // rows
        lax.fori_loop(low, high, take, 0)
        project(xf, (None, rt), (1,), FRONT + at, pl.multiple_of(LEAD + FRONT + at, TILE), chunk)
        for lo, hi in pieces:
            pl.when(at + lo < wanted)(functools.partial(fill, at, lo, hi))

    def owner_left():
        for k in range(3):
            there = me - lift + k - 1 >= 0

            @pl.when(there)
            def _():
                copy_up(k).wait_recv()
                owner_xf[k * rows : (k + 1) * rows, :] = owner_win[k].astype(F32)

            @pl.when(jnp.logical_not(there))
            def _():
                owner_xf[k * rows : (k + 1) * rows, :] = jnp.zeros((rows, channels), F32)

        project(owner_xf, (lt.at[1], None), (0,), -LEAD, 0, near)

    def spread_out(place, lo, hi):
        size_m = hi - lo
        for g, (i0, size) in enumerate(groups):
            depth = WIDE * (4 if size == FIVE else 3)
            masks = None
            if lo < edge:
                end = min(hi, edge) - lo
                offset = lax.broadcasted_iota(jnp.int32, (end, LANES), 0) + (place + lo - i0)
                masks = jnp.where(offset < r, FAR, 0.0).astype(BF16)
                masks = jnp.concatenate([masks] * (depth // LANES), 1) * first_lanes[:, :depth]
                if open_end:
                    tail = jnp.where(offset >= BAND - r, FAR, 0.0).astype(BF16)
                    tail = jnp.concatenate([tail] * (depth // LANES), 1)
                    masks = masks + tail * last_lanes[:, :depth]
            values = []
            for v in range(views):
                value = band[v, lo:hi, :depth].reshape(size_m // TILE, TILE, depth)
                value = value + ltile[g * views + v, :, :depth][None]
                value = value.reshape(size_m, depth)
                if masks is not None:
                    parts = [value[:end] + masks]
                    if end < size_m:
                        parts.append(value[end:])
                    value = jnp.concatenate(parts, 0)
                values.append(jnp.maximum(value, 0))
            term = jnp.maximum(dot(jnp.concatenate(values, 0), wall[:depth]) + bias, 0.0)
            hidden = term[:size_m]
            for v in range(1, views):
                hidden = hidden + term[v * size_m : (v + 1) * size_m]
            hid[lo:hi, g * WIDE : (g + 1) * WIDE] = hidden.astype(BF16)

    def settle(at, place, lo, hi):
        spread_out(place, lo, hi)
        cols[pl.ds(at + lo, hi - lo), :] = dot(hid[lo:hi, :], spread[...])

    def give():
        spread_out(lift * rows, *pieces[0])
        result = dot(hid[:PIECE, :], spread[...])
        padded = jnp.concatenate([result, jnp.zeros((back.shape[1] - PIECE, LANES), F32)], 0)
        back[...] = padded.T[:rows]
        copy_back().start()

    wanted = jnp.minimum(span, total + TILE - base)
    count = (wanted + chunk - 1) // chunk
    if owners:
        count = jnp.minimum(count, chunks)

        @pl.when(helper)
        def _():
            build(jnp.int32(0), 0)
            owner_left()
            left_tiles(1, base - lift * rows)
            give()

    left_tiles(0, base)

    def turn(c, _):
        at = pl.multiple_of(c * chunk, TILE)
        if owners:
            pl.when(jnp.logical_not(helper))(lambda: build(c, at))
        else:
            build(c, at)
        for lo, hi in pieces:
            pl.when(at + lo < wanted)(functools.partial(settle, at, at, lo, hi))
        return 0

    lax.fori_loop(0, count, turn, 0)

    lanes = cols.shape[0]
    upright[...] = cols[...].T[:rows]
    if owners:

        @pl.when(me < owners)
        def _():
            copy_back().wait_recv()
            full = far.shape[1]
            padded = jnp.concatenate([far[...], jnp.zeros((rows, lanes - full), F32)], 1)
            start = lift * rows
            column = lax.broadcasted_iota(jnp.int32, (rows, lanes), 1)
            theirs = (column >= start) & (column < start + PIECE)
            upright[...] = jnp.where(theirs, pltpu.roll(padded, start, 1), upright[...])

        @pl.when(helper)
        def _():
            copy_back().wait_send()

        for k in range(3):

            @pl.when(lifts(k))
            def _():
                copy_up(k).wait_send()

    flat = upright[...]
    row = lax.broadcasted_iota(jnp.int32, (rows, LANES), 0)
    moves = jnp.zeros((rows, LANES), jnp.int32)
    for i0, size in groups:
        for o in range(size):
            moves = jnp.where(row - i0 == o * r, i0, moves)
    moves = jnp.concatenate([moves] * (lanes // LANES), axis=1)
    bit = 1
    while bit < rows:
        flat = jnp.where((moves & bit) != 0, pltpu.roll(flat, lanes - bit, 1), flat)
        bit *= 2
    out_ref[...] = flat[:, :BAND] * (1.0 / views)

    @pl.when(me + 1 < segments)
    def _():
        copy(0).wait_send()

    for slot in range(2, reach + 2):

        @pl.when(me - slot + 1 >= 0)
        def _():
            copy(slot).wait_send()


def per_device(
    bins,
    conv_weight,
    conv_bias,
    pair_left,
    pair_right,
    pair_weight,
    pair_bias,
    head,
    shifts,
    flags,
    dilations,
):
    rows, channels = bins.shape
    views = shifts.shape[0]
    pc = pair_left.shape[1]
    segments = lax.axis_size("seg")
    total, span, chunks, owners, blocks = sizes(rows, segments)
    groups = sum(len(starts) for starts in row_groups(rows))
    depth = WIDE * 4
    lanes = -(-max(chunks * CHUNK, BAND + rows) // LANES) * LANES
    filled = LEAD + FRONT + chunks * CHUNK
    wide_piece = -(-PIECE // LANES) * LANES
    vmem = pl.BlockSpec(memory_space=pltpu.VMEM)
    smem = pl.BlockSpec(memory_space=pltpu.SMEM)
    return pl.pallas_call(
        functools.partial(main_kernel, rows, segments),
        out_shape=jax.ShapeDtypeStruct((rows, BAND), F32),
        in_specs=[smem] * 3 + [pl.BlockSpec(memory_space=pl.ANY)] + [vmem] * 7,
        out_specs=vmem,
        scratch_shapes=[
            pltpu.VMEM((blocks, rows, channels), BF16),
            pltpu.VMEM((blocks * rows, channels), F32),
            pltpu.VMEM((3 * channels, 2 * channels), BF16),
            pltpu.VMEM((2, 2 * channels, 2 * 3 * LANES), BF16),
            pltpu.VMEM((depth, WIDE), BF16),
            pltpu.VMEM((2, 2, 3, LEAD + NEAR + 16, LANES), F32),
            pltpu.VMEM((2, 3, filled, LANES), F32),
            pltpu.VMEM((views, depth // LANES, rows, LANES), F32),
            pltpu.VMEM((groups * views, TILE, depth), BF16),
            pltpu.VMEM((views, CHUNK, depth), BF16),
            pltpu.VMEM((CHUNK, groups * WIDE), BF16),
            pltpu.VMEM((groups * WIDE, LANES), BF16),
            pltpu.VMEM((lanes, LANES), F32),
            pltpu.VMEM((rows, lanes), F32),
            pltpu.VMEM((3, rows, channels), BF16),
            pltpu.VMEM((3 * rows, channels), F32),
            pltpu.VMEM((rows, wide_piece), F32),
            pltpu.VMEM((rows, wide_piece), F32),
            pltpu.SemaphoreType.DMA((blocks,)),
            pltpu.SemaphoreType.DMA((blocks,)),
            pltpu.SemaphoreType.DMA,
            pltpu.SemaphoreType.REGULAR,
            pltpu.SemaphoreType.DMA((3,)),
            pltpu.SemaphoreType.DMA((3,)),
            pltpu.SemaphoreType.REGULAR((3,)),
            pltpu.SemaphoreType.DMA,
            pltpu.SemaphoreType.DMA,
        ],
        compiler_params=pltpu.CompilerParams(
            collective_id=0, has_side_effects=True, vmem_limit_bytes=60 * 1024 * 1024
        ),
    )(
        shifts,
        flags,
        dilations,
        bins,
        conv_weight,
        conv_bias.reshape(1, channels),
        pair_left.T,
        pair_right.T,
        pair_weight.reshape(9 * pc, pc),
        pair_bias.reshape(1, pc),
        head.reshape(1, pc),
    )


def solution(mesh):
    placed = (P(("groups", "seg"), None), P(), P(), P(), P(), P(), P(), P(), P(), P(), P())
    return jax.shard_map(
        per_device,
        mesh=mesh,
        in_specs=placed,
        out_specs=P(("groups", "seg"), None),
        check_vma=False,
    )
```

```python
import functools

import jax
import jax.numpy as jnp
from jax import lax
from jax.experimental import pallas as pl
from jax.experimental.pallas import tpu as pltpu
from jax.sharding import PartitionSpec as P

BAND = 512
DMAX = 4
FIVE = 5
THREE = 3
TAPS = FIVE + 2
WIDE = 256
LANES = 128
LEAD = 16
NEAR = 48
HALO = DMAX
TILE = 16
CHUNK = 208
PIECE = 144
FRONT = 32
FAR = -1e30
F32 = jnp.float32
BF16 = jnp.bfloat16
MESH = pl.DeviceIdType.MESH

SLOTS = sorted(
    [(k, b) for k in range(FIVE) for b in range(3)], key=lambda s: (s[0] + s[1], s[0])
) + sorted(
    [(k, b) for k in range(FIVE, TAPS) for b in range(3)], key=lambda s: (s[0] + s[1], s[0])
)


LOADED = (
    "shifts",
    "flags",
    "dilations",
    "conv_weight",
    "conv_bias",
    "pair_left",
    "pair_right",
    "pair_weight",
    "pair_bias",
    "head",
)


def row_groups(rows):
    tables = {}
    for r in range(1, DMAX + 1):
        fives, threes = [], []
        for first in range(min(r, rows)):
            size = -(-(rows - first) // r)
            best = None
            for a in range(size // FIVE + 2):
                b = max(0, -(-(size - FIVE * a) // THREE))
                cost = (FIVE * a + THREE * b != size, 4 * a + 3 * b)
                if best is None or cost < best[0]:
                    best = (cost, a, b)
            at = 0
            for _ in range(best[1]):
                fives.append(first + r * at)
                at += FIVE
            for _ in range(best[2]):
                threes.append(first + r * at)
                at += THREE
        tables[r] = (fives, threes)
    assert all(len(tables[r][n]) == len(tables[1][n]) for r in tables for n in range(2))
    return [list(zip(*[tables[r][n] for r in range(1, DMAX + 1)])) for n in range(2)]


def group_list(rows, r):
    result = []
    for n, size in enumerate((FIVE, THREE)):
        for starts in row_groups(rows)[n]:
            i0 = jnp.int32(starts[0])
            for value in range(2, DMAX + 1):
                i0 = jnp.where(r == value, starts[value - 1], i0)
            result.append((i0, size))
    return result


def dot(a, b, **kw):
    return jnp.dot(a, b, preferred_element_type=F32, **kw)


def dot_t(a, b):
    return lax.dot_general(a, b, (((0,), (0,)), ((), ())), preferred_element_type=F32)


def slot_of(index, size):
    total = jnp.zeros(index.shape, jnp.int32)
    for k in range(1, FIVE):
        total = total + (index >= k * size).astype(jnp.int32)
    return total


def lane_pick(tile, pc, key, load):
    lane = lax.broadcasted_iota(jnp.int32, (1, LANES), 1)
    first = tile * LANES // pc
    last = min((tile * LANES + LANES - 1) // pc, len(SLOTS) - 1)
    loaded = {}
    value, current = None, None
    for p in range(first, last + 1):
        want = key(SLOTS[p])
        if want == current:
            continue
        if want not in loaded:
            loaded[want] = load(want)
        value = loaded[want] if value is None else jnp.where(lane >= p * pc - tile * LANES, loaded[want], value)
        current = want
    return value


def sizes(rows, segments):
    total = rows * segments
    span = min(BAND + rows, total + TILE)
    chunks = -(-span // CHUNK)
    owners = -(-(total + TILE - 2 * CHUNK) // rows)
    far = (segments - owners) * rows
    helped = (
        total <= BAND
        and 0 < owners
        and 2 * owners <= segments - owners
        and far <= 2 * CHUNK
        and span <= far + PIECE
        and total + TILE - far <= PIECE
    )
    if helped:
        chunks = 2
    else:
        owners = 0
    blocks = -(-(rows + FRONT + HALO + chunks * CHUNK) // rows)
    return total, span, chunks, owners, blocks


def main_kernel(
    rows,
    segments,
    x_ref,
    *refs,
):
    given = len(LOADED)
    main_body(rows, segments, x_ref, refs[:given], *refs[given:])


def main_body(
    rows,
    segments,
    x_ref,
    sources,
    out_ref,
    win,
    xf,
    kern,
    wide,
    wall,
    lt,
    rt,
    lrows,
    ltile,
    band,
    hid,
    spread,
    cols,
    upright,
    owner_win,
    owner_xf,
    back,
    far,
    send_sem,
    recv_sem,
    own_sem,
    ready,
    up_send,
    up_recv,
    up_ready,
    back_send,
    back_recv,
    load_sem,
    *loaded,
):
    shifts, flags, dilations, cw_ref, cb_ref, pleft_ref, pright_ref, pw_ref, pb_ref, head_ref = loaded
    channels = win.shape[2]
    pc = pleft_ref.shape[0]
    views = shifts.shape[0]
    total, span, chunks, owners, blocks = sizes(rows, segments)
    chunk = CHUNK
    lift = segments - owners
    me = lax.axis_index("seg")
    base = me * rows
    reach = min(blocks - 2, segments - 1)
    tiles = wall.shape[0] // LANES

    barrier = pltpu.get_barrier_semaphore()
    for step in range(1, reach + 1):

        @pl.when(me + step < segments)
        def _():
            pl.semaphore_signal(barrier, inc=1, device_id={"seg": me + step}, device_id_type=MESH)

    own = pltpu.make_async_copy(x_ref, win.at[1], own_sem)
    own.start()
    loads = [
        pltpu.make_async_copy(source, held, load_sem.at[n])
        for n, (source, held) in enumerate(zip(sources, loaded))
    ]
    for load in loads:
        load.start()
    own.wait()

    @pl.when(me > 0)
    def _():
        pl.semaphore_wait(barrier, jnp.minimum(me, reach))
        pl.semaphore_signal(ready, inc=1, device_id={"seg": me - 1}, device_id_type=MESH)

    def copy_up(k):
        return pltpu.make_async_remote_copy(
            src_ref=win.at[1],
            dst_ref=owner_win.at[k],
            send_sem=up_send.at[k],
            recv_sem=up_recv.at[k],
            device_id={"seg": me - k + 1 + lift},
            device_id_type=MESH,
        )

    def copy_back():
        return pltpu.make_async_remote_copy(
            src_ref=back,
            dst_ref=far,
            send_sem=back_send,
            recv_sem=back_recv,
            device_id={"seg": me - lift},
            device_id_type=MESH,
        )

    helper = (me >= lift) if owners else None
    for k in range(3 if owners else 0):
        other = me - lift + k - 1

        @pl.when(helper & (other >= 0))
        def _():
            pl.semaphore_signal(up_ready.at[k], inc=1, device_id={"seg": other}, device_id_type=MESH)

    def lifts(k):
        return (me - k + 1 >= 0) & (me - k + 1 < owners)

    def copy(slot):
        return pltpu.make_async_remote_copy(
            src_ref=win.at[1],
            dst_ref=win.at[slot],
            send_sem=send_sem.at[slot],
            recv_sem=recv_sem.at[slot],
            device_id={"seg": me - slot + 1},
            device_id_type=MESH,
        )

    first_slots = -(-(rows + FRONT + HALO + chunk) // rows)
    order = [slot for slot in reversed(range(2, reach + 2)) if slot < first_slots]
    order += [slot for slot in reversed(range(2, reach + 2)) if slot >= first_slots]
    for slot in order:

        @pl.when(me - slot + 1 >= 0)
        def _():
            copy(slot).start()

    for load in loads:
        load.wait()
    q = dilations[0]
    r = dilations[1]
    ci = lax.broadcasted_iota(jnp.int32, (channels, channels), 0)
    cj = lax.broadcasted_iota(jnp.int32, (channels, channels), 1)
    mirror = jnp.where(ci + cj == channels - 1, 1.0, 0.0).astype(BF16)
    for t in range(3):
        at = slice(t * channels, (t + 1) * channels)
        kern[at, :channels] = cw_ref[t]
        kern[at, channels:] = dot(mirror, cw_ref[2 - t]).astype(BF16)

    phases = rt.shape[1]
    lane = lax.broadcasted_iota(jnp.int32, (pc, phases * LANES), 1)
    chan = lax.broadcasted_iota(jnp.int32, (pc, phases * LANES), 0)
    repeat = jnp.zeros(lane.shape, F32)
    for k in range(phases * LANES // pc):
        repeat = jnp.where(lane - chan == k * pc, 1.0, repeat)
    repeat = repeat.astype(BF16)
    across = phases * LANES
    for n, side in enumerate((pleft_ref, pright_ref)):
        part = dot_t(side[...], repeat).astype(BF16)
        for f in range(2):
            for h in range(2):
                wide[n, f * channels : (f + 1) * channels, h * across : (h + 1) * across] = (
                    part if f == h else jnp.zeros_like(part)
                )

    lane = lax.broadcasted_iota(jnp.int32, (pc, WIDE), 1)
    chan = lax.broadcasted_iota(jnp.int32, (pc, WIDE), 0)
    spots = [jnp.where(lane - chan == o * pc, 1.0, 0.0) for o in range(FIVE)]
    placed = [dot(pw_ref[...], spots[o].astype(BF16)) for o in range(FIVE)]
    for p, (k, b) in enumerate(SLOTS):
        block = None
        for o in range(FIVE):
            if 0 <= k - o <= 2:
                first = ((k - o) * 3 + b) * pc
                part = placed[o][first : first + pc]
                block = part if block is None else block + part
        wall[p * pc : (p + 1) * pc, :] = block.astype(BF16)
    used = len(SLOTS) * pc
    wall[used:, :] = jnp.zeros((wall.shape[0] - used, WIDE), BF16)

    bias8 = jnp.broadcast_to(pb_ref[...], (8, pc))
    bias = dot(bias8, sum(spots[1:], spots[0]), precision=lax.Precision.HIGHEST)[0:1, :]
    wi = lax.broadcasted_iota(jnp.int32, (WIDE, pc), 0)
    wc = lax.broadcasted_iota(jnp.int32, (WIDE, pc), 1)
    hit = wi == wc
    for o in range(1, FIVE):
        hit = hit | (wi - wc == o * pc)
    untile = jnp.where(hit, 1.0, 0.0).astype(BF16)
    head_b = jnp.broadcast_to(head_ref[...].astype(F32), (LANES, pc)).astype(BF16)
    head_rows = lax.dot_general(
        untile, head_b, (((1,), (1,)), ((), ())), preferred_element_type=F32
    )
    wide_row = lax.broadcasted_iota(jnp.int32, (WIDE, LANES), 0)
    target = lax.broadcasted_iota(jnp.int32, (WIDE, LANES), 1) - r * slot_of(wide_row, pc)
    groups = group_list(rows, r)
    for g, (i0, size) in enumerate(groups):
        mine = (target == i0) & (wide_row < size * pc)
        spread[g * WIDE : (g + 1) * WIDE, :] = jnp.where(mine, head_rows, 0.0).astype(BF16)
    empty = jnp.broadcast_to(jnp.maximum(bias, 0.0) * float(views), (TILE, WIDE)).astype(BF16)
    blank = dot(jnp.concatenate([empty] * len(groups), 1), spread[...])[0:8]
    rest = cols.shape[0]
    cols[...] = jnp.broadcast_to(blank[None], (rest // 8, 8, LANES)).reshape(rest, LANES)

    @pl.when(me + 1 < segments)
    def _():
        pl.semaphore_wait(ready, 1)
        copy(0).start()

    def take(slot, _):
        source = me + slot - 1
        there = (source >= 0) & (source < segments)
        at = pl.ds(pl.multiple_of(slot * rows, rows), rows)

        @pl.when(there & (slot != 1))
        def _():
            copy(slot).wait_recv()

        @pl.when(there)
        def _():
            xf[at, :] = win[slot].astype(F32)

        @pl.when(jnp.logical_not(there))
        def _():
            xf[at, :] = jnp.zeros((rows, channels), F32)

        return 0

    trunk_bias = jnp.concatenate([cb_ref[...]] * 2, 1)

    def project(source, out, side, first, at, count):
        taps = [source[pl.ds(rows + first + (t - 1) * q, count), :] for t in range(3)]
        stacked = jnp.concatenate([t.astype(BF16) for t in taps], axis=1)
        mixed = dot(stacked, kern[...])
        center = jnp.concatenate([taps[1]] * 2, 1)
        feature = (center + jnp.maximum(mixed + trunk_bias, 0.0)).astype(BF16)
        for n in side:
            value = dot(feature, wide[n])
            for f in range(2):
                for p in range(phases):
                    part = (f * phases + p) * LANES
                    out[n][f, p, pl.ds(at, count), :] = value[:, part : part + LANES]

    def send_up(now):
        for k in range(3 if owners else 0):

            @pl.when(lifts(k) & now)
            def _():
                pl.semaphore_wait(up_ready.at[k], 1)
                copy_up(k).start()

    send_up(me >= 2)
    near = LEAD + NEAR
    lax.fori_loop(0, 3, take, 0)
    project(xf, (lt.at[0], rt), (0, 1), -LEAD, 0, near)
    lt[:, :, :, near:, :] = jnp.zeros((2, 2, phases, lt.shape[3] - near, LANES), F32)

    def left_tiles(which, first):
        left_row = lax.broadcasted_iota(jnp.int32, (rows, LANES), 0) + first
        for v in range(views):
            for tile in range(tiles):

                def left_at(k):
                    value = lt[which, flags[v], tile % phases, pl.ds(LEAD + k * r + shifts[v], rows), :]
                    row = left_row + k * r
                    return jnp.where((row >= 0) & (row < total), value, FAR)

                lrows[v, tile] = lane_pick(tile, pc, lambda s: s[0] - 1, left_at)
        for g, (i0, size) in enumerate(groups):
            for v in range(views):
                for tile in range(tiles):
                    row = lrows[v, tile, pl.ds(i0, 1), :]
                    ltile[g * views + v, :, tile * LANES : (tile + 1) * LANES] = (
                        jnp.broadcast_to(row, (TILE, LANES)).astype(BF16)
                    )

    send_up(me < 2)

    def tap_lanes(b):
        lanes = lax.broadcasted_iota(jnp.int32, (1, wall.shape[0]), 1)
        value = jnp.zeros(lanes.shape, F32)
        for p, slot in enumerate(SLOTS):
            if slot[1] == b:
                value = jnp.where((lanes >= p * pc) & (lanes < (p + 1) * pc), 1.0, value)
        return value.astype(BF16)

    open_end = total > BAND
    edge = chunk if open_end else NEAR
    first_lanes = tap_lanes(0)
    last_lanes = tap_lanes(2)
    pieces = ((0, PIECE), (PIECE, chunk))

    def fill(at, lo, hi):
        size_m = hi - lo
        column = lax.broadcasted_iota(jnp.int32, (size_m, LANES), 0) + (at + lo + base)
        for tile in range(tiles):
            reach_m = lane_pick(tile, pc, lambda s: s[0] + s[1] - 2, lambda s: total - s * r)
            known = column < reach_m
            for v in range(views):
                value = lane_pick(
                    tile,
                    pc,
                    lambda s: s[0] + s[1] - 2,
                    lambda s: rt[
                        flags[v],
                        tile % phases,
                        pl.ds(LEAD + at + lo + s * r + shifts[v], size_m),
                        :,
                    ],
                )
                band[v, lo:hi, tile * LANES : (tile + 1) * LANES] = jnp.where(
                    known, value, FAR
                ).astype(BF16)

    def build(c, at):
        low = jnp.where(c == 0, 3, (rows + FRONT + HALO + c * chunk + rows - 1) // rows)
        high = (rows + FRONT + HALO + (c + 1) * chunk + rows - 1) // rows
        lax.fori_loop(low, high, take, 0)
        project(xf, (None, rt), (1,), FRONT + at, pl.multiple_of(LEAD + FRONT + at, TILE), chunk)
        for lo, hi in pieces:
            pl.when(at + lo < wanted)(functools.partial(fill, at, lo, hi))

    def owner_left():
        for k in range(3):
            there = me - lift + k - 1 >= 0

            @pl.when(there)
            def _():
                copy_up(k).wait_recv()
                owner_xf[k * rows : (k + 1) * rows, :] = owner_win[k].astype(F32)

            @pl.when(jnp.logical_not(there))
            def _():
                owner_xf[k * rows : (k + 1) * rows, :] = jnp.zeros((rows, channels), F32)

        project(owner_xf, (lt.at[1], None), (0,), -LEAD, 0, near)

    def spread_out(place, lo, hi):
        size_m = hi - lo
        for g, (i0, size) in enumerate(groups):
            depth = WIDE * (4 if size == FIVE else 3)
            masks = None
            if lo < edge:
                end = min(hi, edge) - lo
                offset = lax.broadcasted_iota(jnp.int32, (end, LANES), 0) + (place + lo - i0)
                masks = jnp.where(offset < r, FAR, 0.0).astype(BF16)
                masks = jnp.concatenate([masks] * (depth // LANES), 1) * first_lanes[:, :depth]
                if open_end:
                    tail = jnp.where(offset >= BAND - r, FAR, 0.0).astype(BF16)
                    tail = jnp.concatenate([tail] * (depth // LANES), 1)
                    masks = masks + tail * last_lanes[:, :depth]
            values = []
            for v in range(views):
                value = band[v, lo:hi, :depth].reshape(size_m // TILE, TILE, depth)
                value = value + ltile[g * views + v, :, :depth][None]
                value = value.reshape(size_m, depth)
                if masks is not None:
                    parts = [value[:end] + masks]
                    if end < size_m:
                        parts.append(value[end:])
                    value = jnp.concatenate(parts, 0)
                values.append(jnp.maximum(value, 0))
            term = jnp.maximum(dot(jnp.concatenate(values, 0), wall[:depth]) + bias, 0.0)
            hidden = term[:size_m]
            for v in range(1, views):
                hidden = hidden + term[v * size_m : (v + 1) * size_m]
            hid[lo:hi, g * WIDE : (g + 1) * WIDE] = hidden.astype(BF16)

    def settle(at, place, lo, hi):
        spread_out(place, lo, hi)
        cols[pl.ds(at + lo, hi - lo), :] = dot(hid[lo:hi, :], spread[...])

    def give():
        spread_out(lift * rows, *pieces[0])
        result = dot(hid[:PIECE, :], spread[...])
        padded = jnp.concatenate([result, jnp.zeros((back.shape[1] - PIECE, LANES), F32)], 0)
        back[...] = padded.T[:rows]
        copy_back().start()

    wanted = jnp.minimum(span, total + TILE - base)
    count = (wanted + chunk - 1) // chunk
    if owners:
        count = jnp.minimum(count, chunks)

        @pl.when(helper)
        def _():
            build(jnp.int32(0), 0)
            owner_left()
            left_tiles(1, base - lift * rows)
            give()

    left_tiles(0, base)

    def turn(c, _):
        at = pl.multiple_of(c * chunk, TILE)
        if owners:
            pl.when(jnp.logical_not(helper))(lambda: build(c, at))
        else:
            build(c, at)
        for lo, hi in pieces:
            pl.when(at + lo < wanted)(functools.partial(settle, at, at, lo, hi))
        return 0

    lax.fori_loop(0, count, turn, 0)

    lanes = cols.shape[0]
    upright[...] = cols[...].T[:rows]
    if owners:

        @pl.when(me < owners)
        def _():
            copy_back().wait_recv()
            full = far.shape[1]
            padded = jnp.concatenate([far[...], jnp.zeros((rows, lanes - full), F32)], 1)
            start = lift * rows
            column = lax.broadcasted_iota(jnp.int32, (rows, lanes), 1)
            theirs = (column >= start) & (column < start + PIECE)
            upright[...] = jnp.where(theirs, pltpu.roll(padded, start, 1), upright[...])

        @pl.when(helper)
        def _():
            copy_back().wait_send()

        for k in range(3):

            @pl.when(lifts(k))
            def _():
                copy_up(k).wait_send()

    flat = upright[...]
    row = lax.broadcasted_iota(jnp.int32, (rows, LANES), 0)
    moves = jnp.zeros((rows, LANES), jnp.int32)
    for i0, size in groups:
        for o in range(size):
            moves = jnp.where(row - i0 == o * r, i0, moves)
    moves = jnp.concatenate([moves] * (lanes // LANES), axis=1)
    bit = 1
    while bit < rows:
        flat = jnp.where((moves & bit) != 0, pltpu.roll(flat, lanes - bit, 1), flat)
        bit *= 2
    out_ref[...] = flat[:, :BAND]

    @pl.when(me + 1 < segments)
    def _():
        copy(0).wait_send()

    for slot in range(2, reach + 2):

        @pl.when(me - slot + 1 >= 0)
        def _():
            copy(slot).wait_send()


def per_device(
    bins,
    conv_weight,
    conv_bias,
    pair_left,
    pair_right,
    pair_weight,
    pair_bias,
    head,
    shifts,
    flags,
    dilations,
):
    rows, channels = bins.shape
    views = shifts.shape[0]
    pc = pair_left.shape[1]
    segments = lax.axis_size("seg")
    total, span, chunks, owners, blocks = sizes(rows, segments)
    groups = sum(len(starts) for starts in row_groups(rows))
    depth = WIDE * 4
    lanes = -(-max(chunks * CHUNK, BAND + rows) // LANES) * LANES
    filled = LEAD + FRONT + chunks * CHUNK
    wide_piece = -(-PIECE // LANES) * LANES
    vmem = pl.BlockSpec(memory_space=pltpu.VMEM)
    operands = (
        shifts,
        flags,
        dilations,
        conv_weight,
        conv_bias.reshape(1, channels),
        pair_left.T,
        pair_right.T,
        pair_weight.reshape(9 * pc, pc),
        pair_bias.reshape(1, pc),
        head.reshape(1, pc),
    )
    held = [
        (pltpu.SMEM if a.dtype == jnp.int32 else pltpu.VMEM)(a.shape, a.dtype) for a in operands
    ]
    summed = pl.pallas_call(
        functools.partial(main_kernel, rows, segments),
        out_shape=pltpu.VMEM((rows, BAND), F32),
        in_specs=[pl.BlockSpec(memory_space=pl.ANY)] * (1 + len(operands)),
        out_specs=vmem,
        scratch_shapes=[
            pltpu.VMEM((blocks, rows, channels), BF16),
            pltpu.VMEM((blocks * rows, channels), F32),
            pltpu.VMEM((3 * channels, 2 * channels), BF16),
            pltpu.VMEM((2, 2 * channels, 2 * 3 * LANES), BF16),
            pltpu.VMEM((depth, WIDE), BF16),
            pltpu.VMEM((2, 2, 3, LEAD + NEAR + 16, LANES), F32),
            pltpu.VMEM((2, 3, filled, LANES), F32),
            pltpu.VMEM((views, depth // LANES, rows, LANES), F32),
            pltpu.VMEM((groups * views, TILE, depth), BF16),
            pltpu.VMEM((views, CHUNK, depth), BF16),
            pltpu.VMEM((CHUNK, groups * WIDE), BF16),
            pltpu.VMEM((groups * WIDE, LANES), BF16),
            pltpu.VMEM((lanes, LANES), F32),
            pltpu.VMEM((rows, lanes), F32),
            pltpu.VMEM((3, rows, channels), BF16),
            pltpu.VMEM((3 * rows, channels), F32),
            pltpu.VMEM((rows, wide_piece), F32),
            pltpu.VMEM((rows, wide_piece), F32),
            pltpu.SemaphoreType.DMA((blocks,)),
            pltpu.SemaphoreType.DMA((blocks,)),
            pltpu.SemaphoreType.DMA,
            pltpu.SemaphoreType.REGULAR,
            pltpu.SemaphoreType.DMA((3,)),
            pltpu.SemaphoreType.DMA((3,)),
            pltpu.SemaphoreType.REGULAR((3,)),
            pltpu.SemaphoreType.DMA,
            pltpu.SemaphoreType.DMA,
            pltpu.SemaphoreType.DMA((len(operands),)),
            *held,
        ],
        compiler_params=pltpu.CompilerParams(
            collective_id=0, has_side_effects=True, vmem_limit_bytes=58_000_000
        ),
    )(bins, *operands)
    return summed * (1.0 / views)


def solution(mesh):
    placed = (P(("groups", "seg"), None), P(), P(), P(), P(), P(), P(), P(), P(), P(), P())
    return jax.shard_map(
        per_device,
        mesh=mesh,
        in_specs=placed,
        out_specs=P(("groups", "seg"), None),
        check_vma=False,
    )
```

```python
import functools

import jax
import jax.numpy as jnp
from jax import lax
from jax.experimental import pallas as pl
from jax.experimental.pallas import tpu as pltpu
from jax.sharding import PartitionSpec as P

BAND = 512
DMAX = 4
FIVE = 5
THREE = 3
TAPS = FIVE + 2
WIDE = 256
LANES = 128
LEAD = 16
NEAR = 48
HALO = DMAX
TILE = 16
CHUNK = 208
PIECE = 192
FRONT = 32
FAR = -1e30
F32 = jnp.float32
BF16 = jnp.bfloat16
MESH = pl.DeviceIdType.MESH

SLOTS = sorted(
    [(k, b) for k in range(FIVE) for b in range(3)], key=lambda s: (s[0] + s[1], s[0])
) + sorted(
    [(k, b) for k in range(FIVE, TAPS) for b in range(3)], key=lambda s: (s[0] + s[1], s[0])
)


LOADED = (
    "shifts",
    "flags",
    "dilations",
    "conv_weight",
    "conv_bias",
    "pair_left",
    "pair_right",
    "pair_weight",
    "pair_bias",
    "head",
)


def row_groups(rows):
    tables = {}
    for r in range(1, DMAX + 1):
        fives, threes = [], []
        for first in range(min(r, rows)):
            size = -(-(rows - first) // r)
            best = None
            for a in range(size // FIVE + 2):
                b = max(0, -(-(size - FIVE * a) // THREE))
                cost = (FIVE * a + THREE * b != size, 4 * a + 3 * b)
                if best is None or cost < best[0]:
                    best = (cost, a, b)
            at = 0
            for _ in range(best[1]):
                fives.append(first + r * at)
                at += FIVE
            for _ in range(best[2]):
                threes.append(first + r * at)
                at += THREE
        tables[r] = (fives, threes)
    assert all(len(tables[r][n]) == len(tables[1][n]) for r in tables for n in range(2))
    return [list(zip(*[tables[r][n] for r in range(1, DMAX + 1)])) for n in range(2)]


def group_list(rows, r):
    result = []
    for n, size in enumerate((FIVE, THREE)):
        for starts in row_groups(rows)[n]:
            i0 = jnp.int32(starts[0])
            for value in range(2, DMAX + 1):
                i0 = jnp.where(r == value, starts[value - 1], i0)
            result.append((i0, size))
    return result


def dot(a, b, **kw):
    return jnp.dot(a, b, preferred_element_type=F32, **kw)


def dot_t(a, b):
    return lax.dot_general(a, b, (((0,), (0,)), ((), ())), preferred_element_type=F32)


def slot_of(index, size):
    total = jnp.zeros(index.shape, jnp.int32)
    for k in range(1, FIVE):
        total = total + (index >= k * size).astype(jnp.int32)
    return total


def lane_pick(tile, pc, key, load):
    lane = lax.broadcasted_iota(jnp.int32, (1, LANES), 1)
    first = tile * LANES // pc
    last = min((tile * LANES + LANES - 1) // pc, len(SLOTS) - 1)
    loaded = {}
    value, current = None, None
    for p in range(first, last + 1):
        want = key(SLOTS[p])
        if want == current:
            continue
        if want not in loaded:
            loaded[want] = load(want)
        value = loaded[want] if value is None else jnp.where(lane >= p * pc - tile * LANES, loaded[want], value)
        current = want
    return value


def sizes(rows, segments):
    total = rows * segments
    span = min(BAND + rows, total + TILE)
    chunks = 2 if helpers(rows, segments) else -(-span // CHUNK)
    blocks = -(-(rows + FRONT + HALO + chunks * CHUNK) // rows)
    return total, span, chunks, blocks


def helpers(rows, segments):
    total = rows * segments
    span = min(BAND + rows, total + TILE)
    limit = CHUNK + PIECE
    owners = -(-(total + TILE - limit) // rows)
    lift = -(-(max(span, total + TILE) - CHUNK) // rows)
    if total > BAND or owners < 1 or lift * rows > limit or (limit - lift * rows) % TILE:
        return None
    if owners + 1 >= lift or lift + owners > segments or span - lift * rows > CHUNK:
        return None
    return owners, lift, limit


def main_kernel(
    rows,
    segments,
    x_ref,
    *refs,
):
    given = len(LOADED)
    main_body(rows, segments, x_ref, refs[:given], *refs[given:])


def main_body(
    rows,
    segments,
    x_ref,
    sources,
    out_ref,
    win,
    xf,
    kern,
    wide,
    wall,
    lt,
    rt,
    lrows,
    ltile,
    band,
    hid,
    spread,
    cols,
    upright,
    owner_win,
    owner_xf,
    back,
    far,
    send_sem,
    recv_sem,
    own_sem,
    ready,
    up_send,
    up_recv,
    up_ready,
    back_send,
    back_recv,
    load_sem,
    *loaded,
):
    shifts, flags, dilations, cw_ref, cb_ref, pleft_ref, pright_ref, pw_ref, pb_ref, head_ref = loaded
    channels = win.shape[2]
    pc = pleft_ref.shape[0]
    views = shifts.shape[0]
    total, span, chunks, blocks = sizes(rows, segments)
    chunk = CHUNK
    owners, lift, limit = helpers(rows, segments) or (0, 0, 0)
    from_col, to_col = limit - lift * rows, span - lift * rows
    me = lax.axis_index("seg")
    base = me * rows
    reach = min(blocks - 2, segments - 1)
    tiles = wall.shape[0] // LANES

    barrier = pltpu.get_barrier_semaphore()
    for step in range(1, reach + 1):

        @pl.when(me + step < segments)
        def _():
            pl.semaphore_signal(barrier, inc=1, device_id={"seg": me + step}, device_id_type=MESH)

    own = pltpu.make_async_copy(x_ref, win.at[1], own_sem)
    own.start()
    loads = [
        pltpu.make_async_copy(source, held, load_sem.at[n])
        for n, (source, held) in enumerate(zip(sources, loaded))
    ]
    for load in loads:
        load.start()
    own.wait()

    @pl.when(me > 0)
    def _():
        pl.semaphore_wait(barrier, jnp.minimum(me, reach))
        pl.semaphore_signal(ready, inc=1, device_id={"seg": me - 1}, device_id_type=MESH)

    def copy_up(k):
        return pltpu.make_async_remote_copy(
            src_ref=win.at[1],
            dst_ref=owner_win.at[k],
            send_sem=up_send.at[k],
            recv_sem=up_recv.at[k],
            device_id={"seg": me - k + 1 + lift},
            device_id_type=MESH,
        )

    def copy_back():
        return pltpu.make_async_remote_copy(
            src_ref=back,
            dst_ref=far,
            send_sem=back_send,
            recv_sem=back_recv,
            device_id={"seg": me - lift},
            device_id_type=MESH,
        )

    helper = (me >= lift) & (me < lift + owners)
    for k in range(3 if owners else 0):
        other = me - lift + k - 1

        @pl.when(helper & (other >= 0))
        def _():
            pl.semaphore_signal(up_ready.at[k], inc=1, device_id={"seg": other}, device_id_type=MESH)

    def lifts(k):
        return (me - k + 1 >= 0) & (me - k + 1 < owners)

    def copy(slot):
        return pltpu.make_async_remote_copy(
            src_ref=win.at[1],
            dst_ref=win.at[slot],
            send_sem=send_sem.at[slot],
            recv_sem=recv_sem.at[slot],
            device_id={"seg": me - slot + 1},
            device_id_type=MESH,
        )

    first_slots = -(-(rows + FRONT + HALO + chunk) // rows)
    order = [slot for slot in reversed(range(2, reach + 2)) if slot < first_slots]
    order += [slot for slot in reversed(range(2, reach + 2)) if slot >= first_slots]
    for slot in order:

        @pl.when(me - slot + 1 >= 0)
        def _():
            copy(slot).start()

    for load in loads:
        load.wait()
    q = dilations[0]
    r = dilations[1]
    ci = lax.broadcasted_iota(jnp.int32, (channels, channels), 0)
    cj = lax.broadcasted_iota(jnp.int32, (channels, channels), 1)
    mirror = jnp.where(ci + cj == channels - 1, 1.0, 0.0).astype(BF16)
    for t in range(3):
        at = slice(t * channels, (t + 1) * channels)
        kern[at, :channels] = cw_ref[t]
        kern[at, channels:] = dot(mirror, cw_ref[2 - t]).astype(BF16)

    phases = rt.shape[1]
    lane = lax.broadcasted_iota(jnp.int32, (pc, phases * LANES), 1)
    chan = lax.broadcasted_iota(jnp.int32, (pc, phases * LANES), 0)
    repeat = jnp.zeros(lane.shape, F32)
    for k in range(phases * LANES // pc):
        repeat = jnp.where(lane - chan == k * pc, 1.0, repeat)
    repeat = repeat.astype(BF16)
    across = phases * LANES
    for n, side in enumerate((pleft_ref, pright_ref)):
        part = dot_t(side[...], repeat).astype(BF16)
        for f in range(2):
            for h in range(2):
                wide[n, f * channels : (f + 1) * channels, h * across : (h + 1) * across] = (
                    part if f == h else jnp.zeros_like(part)
                )

    lane = lax.broadcasted_iota(jnp.int32, (pc, WIDE), 1)
    chan = lax.broadcasted_iota(jnp.int32, (pc, WIDE), 0)
    spots = [jnp.where(lane - chan == o * pc, 1.0, 0.0) for o in range(FIVE)]
    placed = [dot(pw_ref[...], spots[o].astype(BF16)) for o in range(FIVE)]
    for p, (k, b) in enumerate(SLOTS):
        block = None
        for o in range(FIVE):
            if 0 <= k - o <= 2:
                first = ((k - o) * 3 + b) * pc
                part = placed[o][first : first + pc]
                block = part if block is None else block + part
        wall[p * pc : (p + 1) * pc, :] = block.astype(BF16)
    used = len(SLOTS) * pc
    wall[used:, :] = jnp.zeros((wall.shape[0] - used, WIDE), BF16)

    bias8 = jnp.broadcast_to(pb_ref[...], (8, pc))
    bias = dot(bias8, sum(spots[1:], spots[0]), precision=lax.Precision.HIGHEST)[0:1, :]
    wi = lax.broadcasted_iota(jnp.int32, (WIDE, pc), 0)
    wc = lax.broadcasted_iota(jnp.int32, (WIDE, pc), 1)
    hit = wi == wc
    for o in range(1, FIVE):
        hit = hit | (wi - wc == o * pc)
    untile = jnp.where(hit, 1.0, 0.0).astype(BF16)
    head_b = jnp.broadcast_to(head_ref[...].astype(F32), (LANES, pc)).astype(BF16)
    head_rows = lax.dot_general(
        untile, head_b, (((1,), (1,)), ((), ())), preferred_element_type=F32
    )
    wide_row = lax.broadcasted_iota(jnp.int32, (WIDE, LANES), 0)
    target = lax.broadcasted_iota(jnp.int32, (WIDE, LANES), 1) - r * slot_of(wide_row, pc)
    groups = group_list(rows, r)
    for g, (i0, size) in enumerate(groups):
        mine = (target == i0) & (wide_row < size * pc)
        spread[g * WIDE : (g + 1) * WIDE, :] = jnp.where(mine, head_rows, 0.0).astype(BF16)
    empty = jnp.broadcast_to(jnp.maximum(bias, 0.0) * float(views), (TILE, WIDE)).astype(BF16)
    blank = dot(jnp.concatenate([empty] * len(groups), 1), spread[...])[0:8]
    rest = cols.shape[0]
    cols[...] = jnp.broadcast_to(blank[None], (rest // 8, 8, LANES)).reshape(rest, LANES)

    @pl.when(me + 1 < segments)
    def _():
        pl.semaphore_wait(ready, 1)
        copy(0).start()

    def take(slot, _):
        source = me + slot - 1
        there = (source >= 0) & (source < segments)
        at = pl.ds(pl.multiple_of(slot * rows, rows), rows)

        @pl.when(there & (slot != 1))
        def _():
            copy(slot).wait_recv()

        @pl.when(there)
        def _():
            xf[at, :] = win[slot].astype(F32)

        @pl.when(jnp.logical_not(there))
        def _():
            xf[at, :] = jnp.zeros((rows, channels), F32)

        return 0

    trunk_bias = jnp.concatenate([cb_ref[...]] * 2, 1)

    def project(source, out, side, first, at, count):
        taps = [source[pl.ds(rows + first + (t - 1) * q, count), :] for t in range(3)]
        stacked = jnp.concatenate([t.astype(BF16) for t in taps], axis=1)
        mixed = dot(stacked, kern[...])
        center = jnp.concatenate([taps[1]] * 2, 1)
        feature = (center + jnp.maximum(mixed + trunk_bias, 0.0)).astype(BF16)
        for n in side:
            value = dot(feature, wide[n])
            for f in range(2):
                for p in range(phases):
                    part = (f * phases + p) * LANES
                    out[n][f, p, pl.ds(at, count), :] = value[:, part : part + LANES]

    def send_up(now):
        for k in reversed(range(3 if owners else 0)):

            @pl.when(lifts(k) & now(k))
            def _():
                pl.semaphore_wait(up_ready.at[k], 1)
                copy_up(k).start()

    near = LEAD + NEAR
    lax.fori_loop(0, 3, take, 0)
    project(xf, (lt.at[0], rt), (0, 1), -LEAD, 0, near)
    lt[:, :, :, near:, :] = jnp.zeros((2, 2, phases, lt.shape[3] - near, LANES), F32)

    def left_tiles(which, first):
        left_row = lax.broadcasted_iota(jnp.int32, (rows, LANES), 0) + first
        for v in range(views):
            for tile in range(tiles):

                def left_at(k):
                    value = lt[which, flags[v], tile % phases, pl.ds(LEAD + k * r + shifts[v], rows), :]
                    row = left_row + k * r
                    return jnp.where((row >= 0) & (row < total), value, FAR)

                lrows[v, tile] = lane_pick(tile, pc, lambda s: s[0] - 1, left_at)
        for g, (i0, size) in enumerate(groups):
            for v in range(views):
                for tile in range(tiles):
                    row = lrows[v, tile, pl.ds(i0, 1), :]
                    ltile[g * views + v, :, tile * LANES : (tile + 1) * LANES] = (
                        jnp.broadcast_to(row, (TILE, LANES)).astype(BF16)
                    )

    def tap_lanes(b):
        lanes = lax.broadcasted_iota(jnp.int32, (1, wall.shape[0]), 1)
        value = jnp.zeros(lanes.shape, F32)
        for p, slot in enumerate(SLOTS):
            if slot[1] == b:
                value = jnp.where((lanes >= p * pc) & (lanes < (p + 1) * pc), 1.0, value)
        return value.astype(BF16)

    open_end = total > BAND
    edge = chunk if open_end else NEAR
    first_lanes = tap_lanes(0)
    last_lanes = tap_lanes(2)

    def fill(at, lo, hi):
        size_m = hi - lo
        column = lax.broadcasted_iota(jnp.int32, (size_m, LANES), 0) + (at + lo + base)
        for tile in range(tiles):
            reach_m = lane_pick(tile, pc, lambda s: s[0] + s[1] - 2, lambda s: total - s * r)
            known = column < reach_m
            for v in range(views):
                value = lane_pick(
                    tile,
                    pc,
                    lambda s: s[0] + s[1] - 2,
                    lambda s: rt[
                        flags[v],
                        tile % phases,
                        pl.ds(LEAD + at + lo + s * r + shifts[v], size_m),
                        :,
                    ],
                )
                band[v, lo:hi, tile * LANES : (tile + 1) * LANES] = jnp.where(
                    known, value, FAR
                ).astype(BF16)

    def build(c, at):
        low = jnp.where(c == 0, 3, (rows + FRONT + HALO + c * chunk + rows - 1) // rows)
        high = (rows + FRONT + HALO + (c + 1) * chunk + rows - 1) // rows
        lax.fori_loop(low, high, take, 0)
        project(xf, (None, rt), (1,), FRONT + at, pl.multiple_of(LEAD + FRONT + at, TILE), chunk)
        fill(at, 0, chunk)

    def owner_left():
        for k in range(3):
            there = me - lift + k - 1 >= 0

            @pl.when(there)
            def _():
                copy_up(k).wait_recv()
                owner_xf[k * rows : (k + 1) * rows, :] = owner_win[k].astype(F32)

            @pl.when(jnp.logical_not(there))
            def _():
                owner_xf[k * rows : (k + 1) * rows, :] = jnp.zeros((rows, channels), F32)

        project(owner_xf, (lt.at[1], None), (0,), -LEAD, 0, near)

    def spread_out(place, lo, hi):
        size_m = hi - lo
        for g, (i0, size) in enumerate(groups):
            depth = WIDE * (4 if size == FIVE else 3)
            masks = None
            if not isinstance(place, int) or place + lo < edge:
                end = min(hi, edge) - lo
                offset = lax.broadcasted_iota(jnp.int32, (end, LANES), 0) + (place + lo - i0)
                masks = jnp.where(offset < r, FAR, 0.0).astype(BF16)
                masks = jnp.concatenate([masks] * (depth // LANES), 1) * first_lanes[:, :depth]
                if open_end:
                    tail = jnp.where(offset >= BAND - r, FAR, 0.0).astype(BF16)
                    tail = jnp.concatenate([tail] * (depth // LANES), 1)
                    masks = masks + tail * last_lanes[:, :depth]
            values = []
            for v in range(views):
                value = band[v, lo:hi, :depth].reshape(size_m // TILE, TILE, depth)
                value = value + ltile[g * views + v, :, :depth][None]
                value = value.reshape(size_m, depth)
                if masks is not None:
                    parts = [value[:end] + masks]
                    if end < size_m:
                        parts.append(value[end:])
                    value = jnp.concatenate(parts, 0)
                values.append(jnp.maximum(value, 0))
            term = jnp.maximum(dot(jnp.concatenate(values, 0), wall[:depth]) + bias, 0.0)
            hidden = term[:size_m]
            for v in range(1, views):
                hidden = hidden + term[v * size_m : (v + 1) * size_m]
            hid[lo:hi, g * WIDE : (g + 1) * WIDE] = hidden.astype(BF16)

    def settle(at, place, lo, hi):
        spread_out(place, lo, hi)
        cols[pl.ds(at + lo, hi - lo), :] = dot(hid[lo:hi, :], spread[...])

    def give():
        spread_out(lift * rows, from_col, to_col)
        result = dot(hid[from_col:to_col, :], spread[...])
        short = back.shape[1] - (to_col - from_col)
        padded = result
        if short:
            padded = jnp.concatenate([result, jnp.zeros((short, LANES), F32)], 0)
        back[...] = padded.T[:rows]
        copy_back().start()

    wanted = jnp.minimum(limit if owners else span, total + TILE - base)
    count = (wanted + chunk - 1) // chunk
    if owners:

        @pl.when(helper)
        def _():
            build(jnp.int32(0), 0)
            owner_left()
            left_tiles(1, base - lift * rows)
            give()

    left_tiles(0, base)
    send_up(lambda k: (me >= 2) | (me - k + 1 < 2))

    if owners:

        @pl.when(jnp.logical_not(helper))
        def _():
            build(jnp.int32(0), 0)
            send_up(lambda k: (me < 2) & (me - k + 1 >= 2))

        settle(0, 0, 0, chunk)

        @pl.when(count > 1)
        def _():
            build(jnp.int32(1), chunk)
            settle(chunk, chunk, 0, PIECE)

    else:

        def turn(c, _):
            at = pl.multiple_of(c * chunk, TILE)
            build(c, at)
            settle(at, at, 0, chunk)
            return 0

        lax.fori_loop(0, count, turn, 0)

    lanes = cols.shape[0]
    upright[...] = cols[...].T[:rows]
    if owners:

        @pl.when(me < owners)
        def _():
            copy_back().wait_recv()
            full = far.shape[1]
            padded = jnp.concatenate([far[...], jnp.zeros((rows, lanes - full), F32)], 1)
            start = limit
            column = lax.broadcasted_iota(jnp.int32, (rows, lanes), 1)
            theirs = (column >= limit) & (column < span)
            upright[...] = jnp.where(theirs, pltpu.roll(padded, start, 1), upright[...])

        @pl.when(helper)
        def _():
            copy_back().wait_send()

        for k in range(3):

            @pl.when(lifts(k))
            def _():
                copy_up(k).wait_send()

    flat = upright[...]
    row = lax.broadcasted_iota(jnp.int32, (rows, LANES), 0)
    moves = jnp.zeros((rows, LANES), jnp.int32)
    for i0, size in groups:
        for o in range(size):
            moves = jnp.where(row - i0 == o * r, i0, moves)
    moves = jnp.concatenate([moves] * (lanes // LANES), axis=1)
    bit = 1
    while bit < rows:
        flat = jnp.where((moves & bit) != 0, pltpu.roll(flat, lanes - bit, 1), flat)
        bit *= 2
    out_ref[...] = flat[:, :BAND]

    @pl.when(me + 1 < segments)
    def _():
        copy(0).wait_send()

    for slot in range(2, reach + 2):

        @pl.when(me - slot + 1 >= 0)
        def _():
            copy(slot).wait_send()


def per_device(
    bins,
    conv_weight,
    conv_bias,
    pair_left,
    pair_right,
    pair_weight,
    pair_bias,
    head,
    shifts,
    flags,
    dilations,
):
    rows, channels = bins.shape
    views = shifts.shape[0]
    pc = pair_left.shape[1]
    segments = lax.axis_size("seg")
    total, span, chunks, blocks = sizes(rows, segments)
    groups = sum(len(starts) for starts in row_groups(rows))
    depth = WIDE * 4
    lanes = -(-max(chunks * CHUNK, BAND + rows) // LANES) * LANES
    filled = LEAD + FRONT + chunks * CHUNK
    limit = (helpers(rows, segments) or (0, 0, span))[2]
    wide_piece = -(-max(span - limit, 1) // LANES) * LANES
    vmem = pl.BlockSpec(memory_space=pltpu.VMEM)
    operands = (
        shifts,
        flags,
        dilations,
        conv_weight,
        conv_bias.reshape(1, channels),
        pair_left.T,
        pair_right.T,
        pair_weight.reshape(9 * pc, pc),
        pair_bias.reshape(1, pc),
        head.reshape(1, pc),
    )
    held = [
        (pltpu.SMEM if a.dtype == jnp.int32 else pltpu.VMEM)(a.shape, a.dtype) for a in operands
    ]
    summed = pl.pallas_call(
        functools.partial(main_kernel, rows, segments),
        out_shape=pltpu.VMEM((rows, BAND), F32),
        in_specs=[pl.BlockSpec(memory_space=pl.ANY)] * (1 + len(operands)),
        out_specs=vmem,
        scratch_shapes=[
            pltpu.VMEM((blocks, rows, channels), BF16),
            pltpu.VMEM((blocks * rows, channels), F32),
            pltpu.VMEM((3 * channels, 2 * channels), BF16),
            pltpu.VMEM((2, 2 * channels, 2 * 3 * LANES), BF16),
            pltpu.VMEM((depth, WIDE), BF16),
            pltpu.VMEM((2, 2, 3, LEAD + NEAR + 16, LANES), F32),
            pltpu.VMEM((2, 3, filled, LANES), F32),
            pltpu.VMEM((views, depth // LANES, rows, LANES), F32),
            pltpu.VMEM((groups * views, TILE, depth), BF16),
            pltpu.VMEM((views, CHUNK, depth), BF16),
            pltpu.VMEM((CHUNK, groups * WIDE), BF16),
            pltpu.VMEM((groups * WIDE, LANES), BF16),
            pltpu.VMEM((lanes, LANES), F32),
            pltpu.VMEM((rows, lanes), F32),
            pltpu.VMEM((3, rows, channels), BF16),
            pltpu.VMEM((3 * rows, channels), F32),
            pltpu.VMEM((rows, wide_piece), F32),
            pltpu.VMEM((rows, wide_piece), F32),
            pltpu.SemaphoreType.DMA((blocks,)),
            pltpu.SemaphoreType.DMA((blocks,)),
            pltpu.SemaphoreType.DMA,
            pltpu.SemaphoreType.REGULAR,
            pltpu.SemaphoreType.DMA((3,)),
            pltpu.SemaphoreType.DMA((3,)),
            pltpu.SemaphoreType.REGULAR((3,)),
            pltpu.SemaphoreType.DMA,
            pltpu.SemaphoreType.DMA,
            pltpu.SemaphoreType.DMA((len(operands),)),
            *held,
        ],
        compiler_params=pltpu.CompilerParams(
            collective_id=0, has_side_effects=True, vmem_limit_bytes=58_000_000
        ),
    )(bins, *operands)
    return summed * (1.0 / views)


def solution(mesh):
    placed = (P(("groups", "seg"), None), P(), P(), P(), P(), P(), P(), P(), P(), P(), P())
    return jax.shard_map(
        per_device,
        mesh=mesh,
        in_specs=placed,
        out_specs=P(("groups", "seg"), None),
        check_vma=False,
    )
```

```python
import functools

import jax
import jax.numpy as jnp
from jax import lax
from jax.experimental import pallas as pl
from jax.experimental.pallas import tpu as pltpu
from jax.sharding import PartitionSpec as P

BAND = 512
DMAX = 4
FIVE = 5
THREE = 3
TAPS = FIVE + 2
WIDE = 256
LANES = 128
LEAD = 16
NEAR = 48
HALO = DMAX
TILE = 16
CHUNK = 208
PIECE = 192
FRONT = 32
FAR = -1e30
F32 = jnp.float32
BF16 = jnp.bfloat16
MESH = pl.DeviceIdType.MESH

SLOTS = sorted(
    [(k, b) for k in range(FIVE) for b in range(3)], key=lambda s: (s[0] + s[1], s[0])
) + sorted(
    [(k, b) for k in range(FIVE, TAPS) for b in range(3)], key=lambda s: (s[0] + s[1], s[0])
)


LOADED = (
    "shifts",
    "flags",
    "dilations",
    "conv_weight",
    "conv_bias",
    "pair_left",
    "pair_right",
    "pair_weight",
    "pair_bias",
    "head",
)


def row_groups(rows):
    tables = {}
    for r in range(1, DMAX + 1):
        fives, threes = [], []
        for first in range(min(r, rows)):
            size = -(-(rows - first) // r)
            best = None
            for a in range(size // FIVE + 2):
                b = max(0, -(-(size - FIVE * a) // THREE))
                cost = (FIVE * a + THREE * b != size, 4 * a + 3 * b)
                if best is None or cost < best[0]:
                    best = (cost, a, b)
            at = 0
            for _ in range(best[1]):
                fives.append(first + r * at)
                at += FIVE
            for _ in range(best[2]):
                threes.append(first + r * at)
                at += THREE
        tables[r] = (fives, threes)
    assert all(len(tables[r][n]) == len(tables[1][n]) for r in tables for n in range(2))
    return [list(zip(*[tables[r][n] for r in range(1, DMAX + 1)])) for n in range(2)]


def group_list(rows, r):
    result = []
    for n, size in enumerate((FIVE, THREE)):
        for starts in row_groups(rows)[n]:
            i0 = jnp.int32(starts[0])
            for value in range(2, DMAX + 1):
                i0 = jnp.where(r == value, starts[value - 1], i0)
            result.append((i0, size))
    return result


def dot(a, b, **kw):
    return jnp.dot(a, b, preferred_element_type=F32, **kw)


def dot_t(a, b):
    return lax.dot_general(a, b, (((0,), (0,)), ((), ())), preferred_element_type=F32)


def slot_of(index, size):
    total = jnp.zeros(index.shape, jnp.int32)
    for k in range(1, FIVE):
        total = total + (index >= k * size).astype(jnp.int32)
    return total


def lane_pick(tile, pc, key, load):
    lane = lax.broadcasted_iota(jnp.int32, (1, LANES), 1)
    first = tile * LANES // pc
    last = min((tile * LANES + LANES - 1) // pc, len(SLOTS) - 1)
    loaded = {}
    value, current = None, None
    for p in range(first, last + 1):
        want = key(SLOTS[p])
        if want == current:
            continue
        if want not in loaded:
            loaded[want] = load(want)
        value = loaded[want] if value is None else jnp.where(lane >= p * pc - tile * LANES, loaded[want], value)
        current = want
    return value


def sizes(rows, segments):
    total = rows * segments
    span = min(BAND + rows, total + TILE)
    chunks = 2 if helpers(rows, segments) else -(-span // CHUNK)
    blocks = -(-(rows + FRONT + HALO + chunks * CHUNK) // rows)
    return total, span, chunks, blocks


def helpers(rows, segments):
    total = rows * segments
    span = min(BAND + rows, total + TILE)
    limit = CHUNK + PIECE
    owners = -(-(total + TILE - limit) // rows)
    lift = -(-(max(span, total + TILE) - CHUNK) // rows)
    if total > BAND or owners < 1 or lift * rows > limit or (limit - lift * rows) % TILE:
        return None
    if owners + 1 >= lift or lift + owners > segments or span - lift * rows > CHUNK:
        return None
    return owners, lift, limit


def main_kernel(
    rows,
    segments,
    x_ref,
    *refs,
):
    given = len(LOADED)
    main_body(rows, segments, x_ref, refs[:given], *refs[given:])


def main_body(
    rows,
    segments,
    x_ref,
    sources,
    out_ref,
    win,
    xf,
    kern,
    wide,
    wall,
    lt,
    rt,
    lrows,
    ltile,
    band,
    hid,
    spread,
    cols,
    upright,
    owner_win,
    owner_xf,
    back,
    far,
    send_sem,
    recv_sem,
    own_sem,
    ready,
    up_send,
    up_recv,
    up_ready,
    back_send,
    back_recv,
    load_sem,
    *loaded,
):
    shifts, flags, dilations, cw_ref, cb_ref, pleft_ref, pright_ref, pw_ref, pb_ref, head_ref = loaded
    channels = win.shape[2]
    pc = pleft_ref.shape[0]
    views = shifts.shape[0]
    total, span, chunks, blocks = sizes(rows, segments)
    chunk = CHUNK
    owners, lift, limit = helpers(rows, segments) or (0, 0, 0)
    from_col, to_col = limit - lift * rows, span - lift * rows
    me = lax.axis_index("seg")
    base = me * rows
    reach = min(blocks - 2, segments - 1)
    tiles = wall.shape[0] // LANES

    barrier = pltpu.get_barrier_semaphore()
    for step in range(1, reach + 1):

        @pl.when(me + step < segments)
        def _():
            pl.semaphore_signal(barrier, inc=1, device_id={"seg": me + step}, device_id_type=MESH)

    own = pltpu.make_async_copy(x_ref, win.at[1], own_sem)
    own.start()
    own.wait()

    @pl.when(me > 0)
    def _():
        pl.semaphore_wait(barrier, jnp.minimum(me, reach))
        pl.semaphore_signal(ready, inc=1, device_id={"seg": me - 1}, device_id_type=MESH)

    def copy_up(k):
        return pltpu.make_async_remote_copy(
            src_ref=win.at[1],
            dst_ref=owner_win.at[k],
            send_sem=up_send.at[k],
            recv_sem=up_recv.at[k],
            device_id={"seg": me - k + 1 + lift},
            device_id_type=MESH,
        )

    def copy_back():
        return pltpu.make_async_remote_copy(
            src_ref=back,
            dst_ref=far,
            send_sem=back_send,
            recv_sem=back_recv,
            device_id={"seg": me - lift},
            device_id_type=MESH,
        )

    helper = (me >= lift) & (me < lift + owners)
    for k in range(3 if owners else 0):
        other = me - lift + k - 1

        @pl.when(helper & (other >= 0))
        def _():
            pl.semaphore_signal(up_ready.at[k], inc=1, device_id={"seg": other}, device_id_type=MESH)

    def lifts(k):
        return (me - k + 1 >= 0) & (me - k + 1 < owners)

    def copy(slot):
        return pltpu.make_async_remote_copy(
            src_ref=win.at[1],
            dst_ref=win.at[slot],
            send_sem=send_sem.at[slot],
            recv_sem=recv_sem.at[slot],
            device_id={"seg": me - slot + 1},
            device_id_type=MESH,
        )

    first_slots = -(-(rows + FRONT + HALO + chunk) // rows)
    order = [slot for slot in reversed(range(2, reach + 2)) if slot < first_slots]
    order += [slot for slot in reversed(range(2, reach + 2)) if slot >= first_slots]
    for slot in order:

        @pl.when(me - slot + 1 >= 0)
        def _():
            copy(slot).start()

    loads = [
        pltpu.make_async_copy(source, held, load_sem.at[n])
        for n, (source, held) in enumerate(zip(sources, loaded))
    ]
    for load in loads:
        load.start()
    for load in loads:
        load.wait()
    q = dilations[0]
    r = dilations[1]
    ci = lax.broadcasted_iota(jnp.int32, (channels, channels), 0)
    cj = lax.broadcasted_iota(jnp.int32, (channels, channels), 1)
    mirror = jnp.where(ci + cj == channels - 1, 1.0, 0.0).astype(BF16)
    for t in range(3):
        at = slice(t * channels, (t + 1) * channels)
        kern[at, :channels] = cw_ref[t]
        kern[at, channels:] = dot(mirror, cw_ref[2 - t]).astype(BF16)

    phases = rt.shape[1]
    lane = lax.broadcasted_iota(jnp.int32, (pc, phases * LANES), 1)
    chan = lax.broadcasted_iota(jnp.int32, (pc, phases * LANES), 0)
    repeat = jnp.zeros(lane.shape, F32)
    for k in range(phases * LANES // pc):
        repeat = jnp.where(lane - chan == k * pc, 1.0, repeat)
    repeat = repeat.astype(BF16)
    across = phases * LANES
    for n, side in enumerate((pleft_ref, pright_ref)):
        part = dot_t(side[...], repeat).astype(BF16)
        for f in range(2):
            for h in range(2):
                wide[n, f * channels : (f + 1) * channels, h * across : (h + 1) * across] = (
                    part if f == h else jnp.zeros_like(part)
                )

    lane = lax.broadcasted_iota(jnp.int32, (pc, WIDE), 1)
    chan = lax.broadcasted_iota(jnp.int32, (pc, WIDE), 0)
    spots = [jnp.where(lane - chan == o * pc, 1.0, 0.0) for o in range(FIVE)]
    placed = [dot(pw_ref[...], spots[o].astype(BF16)) for o in range(FIVE)]
    for p, (k, b) in enumerate(SLOTS):
        block = None
        for o in range(FIVE):
            if 0 <= k - o <= 2:
                first = ((k - o) * 3 + b) * pc
                part = placed[o][first : first + pc]
                block = part if block is None else block + part
        wall[p * pc : (p + 1) * pc, :] = block.astype(BF16)
    used = len(SLOTS) * pc
    wall[used:, :] = jnp.zeros((wall.shape[0] - used, WIDE), BF16)

    bias8 = jnp.broadcast_to(pb_ref[...], (8, pc))
    bias = dot(bias8, sum(spots[1:], spots[0]), precision=lax.Precision.HIGHEST)[0:1, :]
    wi = lax.broadcasted_iota(jnp.int32, (WIDE, pc), 0)
    wc = lax.broadcasted_iota(jnp.int32, (WIDE, pc), 1)
    hit = wi == wc
    for o in range(1, FIVE):
        hit = hit | (wi - wc == o * pc)
    untile = jnp.where(hit, 1.0, 0.0).astype(BF16)
    head_b = jnp.broadcast_to(head_ref[...].astype(F32), (LANES, pc)).astype(BF16)
    head_rows = lax.dot_general(
        untile, head_b, (((1,), (1,)), ((), ())), preferred_element_type=F32
    )
    wide_row = lax.broadcasted_iota(jnp.int32, (WIDE, LANES), 0)
    target = lax.broadcasted_iota(jnp.int32, (WIDE, LANES), 1) - r * slot_of(wide_row, pc)
    groups = group_list(rows, r)
    for g, (i0, size) in enumerate(groups):
        mine = (target == i0) & (wide_row < size * pc)
        spread[g * WIDE : (g + 1) * WIDE, :] = jnp.where(mine, head_rows, 0.0).astype(BF16)
    empty = jnp.broadcast_to(jnp.maximum(bias, 0.0) * float(views), (TILE, WIDE)).astype(BF16)
    blank = dot(jnp.concatenate([empty] * len(groups), 1), spread[...])[0:8]
    rest = cols.shape[0]
    cols[...] = jnp.broadcast_to(blank[None], (rest // 8, 8, LANES)).reshape(rest, LANES)

    @pl.when(me + 1 < segments)
    def _():
        pl.semaphore_wait(ready, 1)
        copy(0).start()

    def take(slot, _):
        source = me + slot - 1
        there = (source >= 0) & (source < segments)
        at = pl.ds(pl.multiple_of(slot * rows, rows), rows)

        @pl.when(there & (slot != 1))
        def _():
            copy(slot).wait_recv()

        @pl.when(there)
        def _():
            xf[at, :] = win[slot].astype(F32)

        @pl.when(jnp.logical_not(there))
        def _():
            xf[at, :] = jnp.zeros((rows, channels), F32)

        return 0

    trunk_bias = jnp.concatenate([cb_ref[...]] * 2, 1)

    def project(source, out, side, first, at, count):
        taps = [source[pl.ds(rows + first + (t - 1) * q, count), :] for t in range(3)]
        stacked = jnp.concatenate([t.astype(BF16) for t in taps], axis=1)
        mixed = dot(stacked, kern[...])
        center = jnp.concatenate([taps[1]] * 2, 1)
        feature = (center + jnp.maximum(mixed + trunk_bias, 0.0)).astype(BF16)
        for n in side:
            value = dot(feature, wide[n])
            for f in range(2):
                for p in range(phases):
                    part = (f * phases + p) * LANES
                    out[n][f, p, pl.ds(at, count), :] = value[:, part : part + LANES]

    def send_up(now):
        for k in reversed(range(3 if owners else 0)):

            @pl.when(lifts(k) & now(k))
            def _():
                pl.semaphore_wait(up_ready.at[k], 1)
                copy_up(k).start()

    near = LEAD + NEAR
    lax.fori_loop(0, 3, take, 0)
    project(xf, (lt.at[0], rt), (0, 1), -LEAD, 0, near)
    lt[:, :, :, near:, :] = jnp.zeros((2, 2, phases, lt.shape[3] - near, LANES), F32)

    def left_tiles(which, first):
        left_row = lax.broadcasted_iota(jnp.int32, (rows, LANES), 0) + first
        for v in range(views):
            for tile in range(tiles):

                def left_at(k):
                    value = lt[which, flags[v], tile % phases, pl.ds(LEAD + k * r + shifts[v], rows), :]
                    row = left_row + k * r
                    return jnp.where((row >= 0) & (row < total), value, FAR)

                lrows[v, tile] = lane_pick(tile, pc, lambda s: s[0] - 1, left_at)
        for g, (i0, size) in enumerate(groups):
            for v in range(views):
                for tile in range(tiles):
                    row = lrows[v, tile, pl.ds(i0, 1), :]
                    ltile[g * views + v, :, tile * LANES : (tile + 1) * LANES] = (
                        jnp.broadcast_to(row, (TILE, LANES)).astype(BF16)
                    )

    def tap_lanes(b):
        lanes = lax.broadcasted_iota(jnp.int32, (1, wall.shape[0]), 1)
        value = jnp.zeros(lanes.shape, F32)
        for p, slot in enumerate(SLOTS):
            if slot[1] == b:
                value = jnp.where((lanes >= p * pc) & (lanes < (p + 1) * pc), 1.0, value)
        return value.astype(BF16)

    open_end = total > BAND
    edge = chunk if open_end else NEAR
    first_lanes = tap_lanes(0)
    last_lanes = tap_lanes(2)

    def fill(at, lo, hi):
        size_m = hi - lo
        column = lax.broadcasted_iota(jnp.int32, (size_m, LANES), 0) + (at + lo + base)
        for tile in range(tiles):
            reach_m = lane_pick(tile, pc, lambda s: s[0] + s[1] - 2, lambda s: total - s * r)
            known = column < reach_m
            for v in range(views):
                value = lane_pick(
                    tile,
                    pc,
                    lambda s: s[0] + s[1] - 2,
                    lambda s: rt[
                        flags[v],
                        tile % phases,
                        pl.ds(LEAD + at + lo + s * r + shifts[v], size_m),
                        :,
                    ],
                )
                band[v, lo:hi, tile * LANES : (tile + 1) * LANES] = jnp.where(
                    known, value, FAR
                ).astype(BF16)

    def build(c, at, lo=0):
        low = jnp.where(c == 0, 3, (rows + FRONT + HALO + c * chunk + rows - 1) // rows)
        high = (rows + FRONT + HALO + (c + 1) * chunk + rows - 1) // rows
        lax.fori_loop(low, high, take, 0)
        project(xf, (None, rt), (1,), FRONT + at, pl.multiple_of(LEAD + FRONT + at, TILE), chunk)
        fill(at, lo, chunk)

    def owner_left():
        for k in range(3):
            there = me - lift + k - 1 >= 0

            @pl.when(there)
            def _():
                copy_up(k).wait_recv()
                owner_xf[k * rows : (k + 1) * rows, :] = owner_win[k].astype(F32)

            @pl.when(jnp.logical_not(there))
            def _():
                owner_xf[k * rows : (k + 1) * rows, :] = jnp.zeros((rows, channels), F32)

        project(owner_xf, (lt.at[1], None), (0,), -LEAD, 0, near)

    def spread_out(place, lo, hi):
        size_m = hi - lo
        for g, (i0, size) in enumerate(groups):
            depth = WIDE * (4 if size == FIVE else 3)
            masks = None
            if not isinstance(place, int) or place + lo < edge:
                end = min(hi, edge) - lo
                offset = lax.broadcasted_iota(jnp.int32, (end, LANES), 0) + (place + lo - i0)
                masks = jnp.where(offset < r, FAR, 0.0).astype(BF16)
                masks = jnp.concatenate([masks] * (depth // LANES), 1) * first_lanes[:, :depth]
                if open_end:
                    tail = jnp.where(offset >= BAND - r, FAR, 0.0).astype(BF16)
                    tail = jnp.concatenate([tail] * (depth // LANES), 1)
                    masks = masks + tail * last_lanes[:, :depth]
            values = []
            for v in range(views):
                value = band[v, lo:hi, :depth].reshape(size_m // TILE, TILE, depth)
                value = value + ltile[g * views + v, :, :depth][None]
                value = value.reshape(size_m, depth)
                if masks is not None:
                    parts = [value[:end] + masks]
                    if end < size_m:
                        parts.append(value[end:])
                    value = jnp.concatenate(parts, 0)
                values.append(jnp.maximum(value, 0))
            term = jnp.maximum(dot(jnp.concatenate(values, 0), wall[:depth]) + bias, 0.0)
            hidden = term[:size_m]
            for v in range(1, views):
                hidden = hidden + term[v * size_m : (v + 1) * size_m]
            hid[lo:hi, g * WIDE : (g + 1) * WIDE] = hidden.astype(BF16)

    def settle(at, place, lo, hi):
        spread_out(place, lo, hi)
        cols[pl.ds(at + lo, hi - lo), :] = dot(hid[lo:hi, :], spread[...])

    def give():
        spread_out(lift * rows, from_col, to_col)
        result = dot(hid[from_col:to_col, :], spread[...])
        short = back.shape[1] - (to_col - from_col)
        padded = result
        if short:
            padded = jnp.concatenate([result, jnp.zeros((short, LANES), F32)], 0)
        back[...] = padded.T[:rows]
        copy_back().start()

    wanted = jnp.minimum(limit if owners else span, total + TILE - base)
    count = (wanted + chunk - 1) // chunk
    if owners:

        @pl.when(helper)
        def _():
            build(jnp.int32(0), 0, from_col)
            owner_left()
            left_tiles(1, base - lift * rows)
            give()
            fill(0, 0, from_col)

    left_tiles(0, base)
    send_up(lambda k: (me >= 2) | (me - k + 1 < 2))

    if owners:

        @pl.when(jnp.logical_not(helper))
        def _():
            build(jnp.int32(0), 0)
            send_up(lambda k: (me < 2) & (me - k + 1 >= 2))

        settle(0, 0, 0, chunk)

        @pl.when(count > 1)
        def _():
            build(jnp.int32(1), chunk)
            settle(chunk, chunk, 0, PIECE)

    else:

        def turn(c, _):
            at = pl.multiple_of(c * chunk, TILE)
            build(c, at)
            settle(at, at, 0, chunk)
            return 0

        lax.fori_loop(0, count, turn, 0)

    lanes = cols.shape[0]
    upright[...] = cols[...].T[:rows]
    if owners:

        @pl.when(me < owners)
        def _():
            copy_back().wait_recv()
            full = far.shape[1]
            padded = jnp.concatenate([far[...], jnp.zeros((rows, lanes - full), F32)], 1)
            start = limit
            column = lax.broadcasted_iota(jnp.int32, (rows, lanes), 1)
            theirs = (column >= limit) & (column < span)
            upright[...] = jnp.where(theirs, pltpu.roll(padded, start, 1), upright[...])

        @pl.when(helper)
        def _():
            copy_back().wait_send()

        for k in range(3):

            @pl.when(lifts(k))
            def _():
                copy_up(k).wait_send()

    flat = upright[...]
    row = lax.broadcasted_iota(jnp.int32, (rows, LANES), 0)
    moves = jnp.zeros((rows, LANES), jnp.int32)
    for i0, size in groups:
        for o in range(size):
            moves = jnp.where(row - i0 == o * r, i0, moves)
    moves = jnp.concatenate([moves] * (lanes // LANES), axis=1)
    bit = 1
    while bit < rows:
        flat = jnp.where((moves & bit) != 0, pltpu.roll(flat, lanes - bit, 1), flat)
        bit *= 2
    out_ref[...] = flat[:, :BAND]

    @pl.when(me + 1 < segments)
    def _():
        copy(0).wait_send()

    for slot in range(2, reach + 2):

        @pl.when(me - slot + 1 >= 0)
        def _():
            copy(slot).wait_send()


def per_device(
    bins,
    conv_weight,
    conv_bias,
    pair_left,
    pair_right,
    pair_weight,
    pair_bias,
    head,
    shifts,
    flags,
    dilations,
):
    rows, channels = bins.shape
    views = shifts.shape[0]
    pc = pair_left.shape[1]
    segments = lax.axis_size("seg")
    total, span, chunks, blocks = sizes(rows, segments)
    groups = sum(len(starts) for starts in row_groups(rows))
    depth = WIDE * 4
    lanes = -(-max(chunks * CHUNK, BAND + rows) // LANES) * LANES
    filled = LEAD + FRONT + chunks * CHUNK
    limit = (helpers(rows, segments) or (0, 0, span))[2]
    wide_piece = -(-max(span - limit, 1) // LANES) * LANES
    vmem = pl.BlockSpec(memory_space=pltpu.VMEM)
    operands = (
        shifts,
        flags,
        dilations,
        conv_weight,
        conv_bias.reshape(1, channels),
        pair_left.T,
        pair_right.T,
        pair_weight.reshape(9 * pc, pc),
        pair_bias.reshape(1, pc),
        head.reshape(1, pc),
    )
    held = [
        (pltpu.SMEM if a.dtype == jnp.int32 else pltpu.VMEM)(a.shape, a.dtype) for a in operands
    ]
    summed = pl.pallas_call(
        functools.partial(main_kernel, rows, segments),
        out_shape=pltpu.VMEM((rows, BAND), F32),
        in_specs=[pl.BlockSpec(memory_space=pl.ANY)] * (1 + len(operands)),
        out_specs=vmem,
        scratch_shapes=[
            pltpu.VMEM((blocks, rows, channels), BF16),
            pltpu.VMEM((blocks * rows, channels), F32),
            pltpu.VMEM((3 * channels, 2 * channels), BF16),
            pltpu.VMEM((2, 2 * channels, 2 * 3 * LANES), BF16),
            pltpu.VMEM((depth, WIDE), BF16),
            pltpu.VMEM((2, 2, 3, LEAD + NEAR + 16, LANES), F32),
            pltpu.VMEM((2, 3, filled, LANES), F32),
            pltpu.VMEM((views, depth // LANES, rows, LANES), F32),
            pltpu.VMEM((groups * views, TILE, depth), BF16),
            pltpu.VMEM((views, CHUNK, depth), BF16),
            pltpu.VMEM((CHUNK, groups * WIDE), BF16),
            pltpu.VMEM((groups * WIDE, LANES), BF16),
            pltpu.VMEM((lanes, LANES), F32),
            pltpu.VMEM((rows, lanes), F32),
            pltpu.VMEM((3, rows, channels), BF16),
            pltpu.VMEM((3 * rows, channels), F32),
            pltpu.VMEM((rows, wide_piece), F32),
            pltpu.VMEM((rows, wide_piece), F32),
            pltpu.SemaphoreType.DMA((blocks,)),
            pltpu.SemaphoreType.DMA((blocks,)),
            pltpu.SemaphoreType.DMA,
            pltpu.SemaphoreType.REGULAR,
            pltpu.SemaphoreType.DMA((3,)),
            pltpu.SemaphoreType.DMA((3,)),
            pltpu.SemaphoreType.REGULAR((3,)),
            pltpu.SemaphoreType.DMA,
            pltpu.SemaphoreType.DMA,
            pltpu.SemaphoreType.DMA((len(operands),)),
            *held,
        ],
        compiler_params=pltpu.CompilerParams(
            collective_id=0, has_side_effects=True, vmem_limit_bytes=58_000_000
        ),
    )(bins, *operands)
    return summed * (1.0 / views)


def solution(mesh):
    placed = (P(("groups", "seg"), None), P(), P(), P(), P(), P(), P(), P(), P(), P(), P())
    return jax.shard_map(
        per_device,
        mesh=mesh,
        in_specs=placed,
        out_specs=P(("groups", "seg"), None),
        check_vma=False,
    )
```
